128 devices in a mesh: ax: 32 (over x, y, core), rad: 4 (over z).
Axes of the slice: x: 4, y: 4, z: 4, core: 2. Of those that a mesh axis runs over, the one named last changes fastest.
Arguments:
- couplings: bfloat16 [32, 10, 1728, 1728], P('ax', None, 'rad'), may hold values from -0.071777344 to 0.071777344
- pivots: float32 [32, 1728, 1728], P('ax', 'rad'), may hold values from -0.02946892 to 1.0294689
- pattern: int32 [32, 10, 9, 9], P('ax'), may hold values 0 or 1
- krylov: float32 [32, 32, 1728], P('ax', None, 'rad'), may hold values from -6 to 6
Outputs:
- basis_block: float32 [32, 16, 1728], P('ax', None, 'rad')
- coefficients: float32 [32, 16], replicated
- upper: float32 [16, 16], replicated
The draws below stay inside these ranges and needn't reach their ends.
All inputs are finite; a program needn't handle non-finite values. No bound on the sum of `pattern` on one device may be relied on, other than what follows from the above.
Results may differ from the reference program's by a relative error of at most 0.0003.
Values sent between devices are 32-bit elements; how exact they have to be, the bound alone decides.
No kernel may reach another device: no remote copies, remote signals or barrier semaphores. Data moves between devices by JAX's collectives and lax.ppermute only.
A program may use at most 128 MiB of HBM per device.

```python
import jax
import jax.numpy as jnp
from jax import lax

FIELDS = 9
POINTS = 192
NRHS = 16
KRYLOV = 32
B = 1728
NB = 32
LEVELS = 5
ROWS = 55296


def draw_pivots(key, part):
    identity = jnp.eye(B, dtype=jnp.float32)
    limit = 1.225 / B ** 0.5
    noise = jax.random.normal(key, (NB, B, B), jnp.float32) * (0.7 / B ** 0.5)
    noise = jnp.clip(noise, -limit, limit)
    return identity[None] + noise


def plant(values, rng, low, top_value):
    place = [jax.random.randint(jax.random.fold_in(rng, axis), (), 0, length) for axis, length in enumerate(values.shape)]
    longest = values.shape.index(max(values.shape))
    neighbour = place[:longest] + [(place[longest] + 1) % values.shape[longest]] + place[longest + 1:]
    return values.at[tuple(place)].set(low).at[tuple(neighbour)].set(top_value)


def block_scale(own_key, dims, cuts, low, high):
    def one(axis_at, parts):
        steps = jax.random.uniform(jax.random.fold_in(jax.random.fold_in(own_key, 6), axis_at), (parts,), jnp.float32, low / len(cuts), high / len(cuts))
        return jnp.repeat(jnp.exp(steps), dims[axis_at] // parts).reshape((-1,) + (1,) * (len(dims) - axis_at - 1))

    gain = one(*cuts[0])
    for cut in cuts[1:]:
        gain = gain * one(*cut)
    return gain


def bell_draw(key, dims, spread, reach, cuts=(), held_as=jnp.bfloat16):
    drawn = jax.random.normal(key, dims, jnp.float32) * spread
    if len(cuts) > 0:
        drawn = block_scale(key, dims, cuts, -0.22, 0.18) * drawn
    return jnp.clip(drawn, min=-reach, max=reach).astype(held_as)


def setup_inputs(seed: int = 0) -> dict:
    seeds = jax.random.split(jax.random.key(seed), 5)
    couplings = bell_draw(seeds[0], (NB, 2 * LEVELS, B, B), (0.6 / B ** 0.5), 0.071777344, ((0, 32), (2, 4)))
    pivots = draw_pivots(jax.random.fold_in(seeds[4], 71), 0)
    pattern = plant((jax.random.randint(seeds[2], (NB, 2 * LEVELS, FIELDS, FIELDS), 0, 4) < 3).astype(jnp.int32), jax.random.fold_in(seeds[2], 1), 0, 1)
    krylov = bell_draw(seeds[3], (NB, KRYLOV, B), 1.0, 6.0, ((0, 32), (2, 4)), jnp.float32)
    return dict(couplings=couplings, pivots=pivots, pattern=pattern, krylov=krylov)


precise = lax.Precision.HIGHEST

def expand(mask):
    ones = mask.astype(jnp.float32)
    return jnp.repeat(jnp.repeat(ones, POINTS, axis=0), POINTS, axis=1)

def apply_factor(factor, vectors):
    return jnp.einsum('rc,kc->kr', factor, vectors, precision=precise)

def factor_of(couplings, pattern, block, kind):
    return couplings[block, kind].astype(jnp.float32) * expand(pattern[block, kind])

def reference(couplings, pivots, pattern, krylov):
    residue = krylov[:, KRYLOV - NRHS:, :]
    for rung in range(LEVELS):
        stride = 2 ** rung
        high = jnp.stack([apply_factor(factor_of(couplings, pattern, n, 2 * rung), residue[n]) for n in range(NB)])
        low = jnp.stack([apply_factor(factor_of(couplings, pattern, n, 2 * rung + 1), residue[n]) for n in range(NB)])
        zeros_pad = jnp.zeros((stride, NRHS, B), jnp.float32)
        from_below = jnp.concatenate([zeros_pad, high[:NB - stride]], axis=0)
        from_above = jnp.concatenate([low[stride:], zeros_pad], axis=0)
        residue = residue - from_below - from_above
    stacked = jnp.stack([apply_factor(pivots[n], residue[n]) for n in range(NB)])
    coefficients = jnp.einsum('nkb,nrb->kr', krylov, stacked, precision=precise) / ROWS
    remainder = stacked - jnp.einsum('kr,nkb->nrb', coefficients, krylov, precision=precise)
    gram = jnp.einsum('nrb,nsb->rs', remainder, remainder, precision=precise) / ROWS
    lower = jnp.linalg.cholesky(gram)
    flat = remainder.transpose(1, 0, 2).reshape(NRHS, NB * B)
    solved = lax.linalg.triangular_solve(lower, flat, left_side=True, lower=True)
    basis_block = solved.reshape(NRHS, NB, B).transpose(1, 0, 2)
    return (basis_block, coefficients, lower.T)
```

```python
import functools

import jax
import jax.numpy as jnp
from jax import lax
from jax.experimental import pallas as pl
from jax.experimental.pallas import tpu as pltpu
from jax.sharding import PartitionSpec as P

NRHS = 16
GROUP = 48
precise = lax.Precision.HIGHEST


VMEM = pl.BlockSpec(memory_space=pltpu.VMEM)
SMEM = pl.BlockSpec(memory_space=pltpu.SMEM)
ANY = pl.BlockSpec(memory_space=pl.ANY)


def nt_dot(a, b, precision=None):
    return lax.dot_general(
        a, b, (((1,), (1,)), ((), ())), precision=precision,
        preferred_element_type=jnp.float32,
    )


def nn_dot(a, b, precision=None):
    return lax.dot_general(
        a, b, (((1,), (0,)), ((), ())), precision=precision,
        preferred_element_type=jnp.float32,
    )


def split2(value):
    high = value.astype(jnp.bfloat16)
    low = (value - high.astype(jnp.float32)).astype(jnp.bfloat16)
    return high, low


def prep_kernel(rung, fields, slots, pattern_ref, couplings_ref, _, out_ref, sems):
    block = lax.axis_index("ax")
    rad = lax.axis_index("rad")
    odd = (block // (1 << rung)) % 2
    rows, width = out_ref.shape[1:]
    groups = rows // GROUP
    points = width // fields
    chunk = 3 * GROUP
    copies = []
    for slot in range(slots):
        kind = 2 * rung + (odd if slot == 0 else 1 - odd)
        for part in range(rows // chunk):
            copy = pltpu.make_async_copy(
                couplings_ref.at[0, kind, pl.ds(part * chunk, chunk)],
                out_ref.at[slot, pl.ds(part * chunk, chunk)],
                sems.at[slot, part],
            )
            copy.start()
            copies.append((slot, part, kind, copy))
    col_field = lax.broadcasted_iota(jnp.int32, (8, width), 1) // points
    for slot, part, kind, copy in copies:
        copy.wait()
        for sub in range(3):
            group = part * 3 + sub
            field = (rad * groups + group) * GROUP // points
            keep = jnp.zeros((8, width), jnp.float32)
            for col in range(fields):
                bit = pattern_ref[0, kind, field, col].astype(jnp.float32)
                keep = jnp.where(col_field == col, bit, keep)
            keep = jnp.concatenate([keep, keep], axis=0).astype(jnp.bfloat16)
            for tile in range(GROUP // 16):
                at = pl.ds(group * GROUP + tile * 16, 16)
                out_ref[slot, at, :] = out_ref[slot, at, :] * keep


def prep(rung, slots, pattern, couplings, after):
    rows, width = couplings.shape[2:]
    return pl.pallas_call(
        functools.partial(prep_kernel, rung, pattern.shape[3], slots),
        out_shape=jax.ShapeDtypeStruct((slots, rows, width), jnp.bfloat16),
        in_specs=[SMEM, ANY, ANY],
        out_specs=VMEM,
        scratch_shapes=[pltpu.SemaphoreType.DMA((slots, rows // (3 * GROUP)))],
        name=f"prep{rung}",
    )(pattern, couplings, after)


def pivot_kernel(pivots_ref, _, out_ref, stage, sems):
    rows = pivots_ref.shape[1]
    part = rows // 3
    copies = []
    for i in range(3):
        copy = pltpu.make_async_copy(
            pivots_ref.at[0, pl.ds(i * part, part)], stage.at[pl.ds(i * part, part)], sems.at[i]
        )
        copy.start()
        copies.append(copy)
    for i, copy in enumerate(copies):
        copy.wait()
        for tile in range(part // 16):
            at = pl.ds(i * part + tile * 16, 16)
            high, low = split2(stage[at, :])
            out_ref[0, at, :] = high
            out_ref[1, at, :] = low


def prep_pivots(pivots, after):
    rows, width = pivots.shape[1:]
    return pl.pallas_call(
        pivot_kernel,
        out_shape=jax.ShapeDtypeStruct((2, rows, width), jnp.bfloat16),
        in_specs=[ANY, ANY],
        out_specs=VMEM,
        scratch_shapes=[pltpu.VMEM((rows, width), jnp.float32), pltpu.SemaphoreType.DMA((3,))],
        name="prep_pivots",
    )(pivots, after)


def gram_kernel(stored_ref, out_ref):
    stored = stored_ref[0]
    g = nt_dot(stored, stored, precise)
    out_ref[...] = jnp.concatenate([g[8 * i : 8 * i + 8] for i in range(4)], axis=1)


def stored_gram(krylov):
    return pl.pallas_call(
        gram_kernel,
        out_shape=jax.ShapeDtypeStruct((8, 128), jnp.float32),
        in_specs=[VMEM],
        out_specs=VMEM,
        name="stored_gram",
    )(krylov)


def gather_rows(slices, whole):
    rad = lax.axis_index("rad")
    for m, piece in enumerate(slices):
        whole[rad ^ m] = piece[:NRHS, :]
    v = jnp.concatenate([whole[t] for t in range(4)], axis=1)
    return jnp.concatenate(split2(v), axis=0)


def level_kernel(slots, s0, s1, s2, s3, w_ref, g_ref, *rest):
    outs, whole = rest[:-1], rest[-1]
    lhs = gather_rows((s0, s1, s2, s3), whole)
    for slot in range(slots):
        both = nt_dot(lhs, w_ref[slot])
        outs[slot][:NRHS, :] = both[:NRHS] + both[NRHS:]
    outs[0][NRHS:, :128] = g_ref[...]
    outs[0][NRHS:, 128:] = jnp.zeros((8, outs[0].shape[1] - 128), jnp.float32)


def level(slots, slices, weights, g):
    rows = weights.shape[1]
    shapes = [(NRHS + 8, rows), (NRHS, rows)][:slots]
    return pl.pallas_call(
        functools.partial(level_kernel, slots),
        out_shape=[jax.ShapeDtypeStruct(s, jnp.float32) for s in shapes],
        in_specs=[VMEM] * 6,
        out_specs=[VMEM] * slots,
        scratch_shapes=[pltpu.VMEM((4, NRHS, rows), jnp.float32)],
        name="level",
    )(*slices, weights, g)


def solve_kernel(s0, s1, s2, s3, p_ref, stored_ref, x_ref, part_ref, g_ref, whole, gs):
    rad = lax.axis_index("rad")
    lhs = gather_rows((s0, s1, s2, s3), whole)
    both = nt_dot(lhs, p_ref[0])
    x = both[:NRHS] + both[NRHS:] + nt_dot(lhs[:NRHS], p_ref[1])
    x_ref[...] = x
    t = jnp.concatenate(
        [nt_dot(x, stored_ref[0], precise), nt_dot(x, x, precise)], axis=1
    )
    part_ref[...] = jnp.concatenate(
        [t[:8], t[8:], jnp.zeros((8, 32), jnp.float32)], axis=1
    )
    for m, piece in enumerate((s0, s1, s2, s3)):
        gs[rad ^ m] = piece[NRHS:, :128]
    g_ref[...] = (gs[0] + gs[1]) + (gs[2] + gs[3])


def solve(slices, pivots, krylov):
    rows = pivots.shape[1]
    return pl.pallas_call(
        solve_kernel,
        out_shape=[
            jax.ShapeDtypeStruct((NRHS, rows), jnp.float32),
            jax.ShapeDtypeStruct((8, 128), jnp.float32),
            jax.ShapeDtypeStruct((8, 128), jnp.float32),
        ],
        in_specs=[VMEM] * 6,
        out_specs=[VMEM] * 3,
        scratch_shapes=[
            pltpu.VMEM((4, NRHS, rows), jnp.float32),
            pltpu.VMEM((4, 8, 128), jnp.float32),
        ],
        name="solve",
    )(*slices, pivots, krylov)


def finish_kernel(total, parts_ref, g_ref, x_ref, stored_ref, basis_ref, coef_ref, upper_ref):
    s = jnp.sum(parts_ref[...], axis=0) * (1.0 / total)
    t = jnp.concatenate([s[:, :48], s[:, 48:96]], axis=0)
    gs = g_ref[...] * (1.0 / total)
    g = jnp.concatenate([gs[:, 32 * i : 32 * i + 32] for i in range(4)], axis=0)
    ct = t[:, :32]
    xx = t[:, 32:48]
    coef_ref[...] = ct.T
    stored = stored_ref[0]
    remainder = x_ref[...] - nn_dot(ct, stored, precise)
    gram = xx - nt_dot(2.0 * ct - nn_dot(ct, g, precise), ct, precise)
    row = lax.broadcasted_iota(jnp.int32, (NRHS, 2 * NRHS), 0)
    col = lax.broadcasted_iota(jnp.int32, (NRHS, 2 * NRHS), 1)
    eye = (lax.broadcasted_iota(jnp.int32, (NRHS, NRHS), 0)
           == lax.broadcasted_iota(jnp.int32, (NRHS, NRHS), 1)).astype(jnp.float32)
    a = jnp.concatenate([gram, eye], axis=1)
    for k in range(NRHS - 1):
        factor = a[:, k : k + 1] / a[k : k + 1, k : k + 1]
        a = jnp.where(row > k, a - factor * a[k : k + 1, :], a)
    diag = jnp.sum(jnp.where(row == col, a, 0.0), axis=1, keepdims=True)
    a = a * lax.rsqrt(diag)
    u = a[:, :NRHS]
    upper_ref[...] = jnp.where(row[:, :NRHS] <= col[:, :NRHS], u, 0.0)
    basis_ref[0] = nn_dot(a[:, NRHS:], remainder, precise)


def finish(total, parts, g, x, krylov):
    rows = x.shape[1]
    stored = krylov.shape[1]
    return pl.pallas_call(
        functools.partial(finish_kernel, total),
        out_shape=[
            jax.ShapeDtypeStruct((1, NRHS, rows), jnp.float32),
            jax.ShapeDtypeStruct((stored, NRHS), jnp.float32),
            jax.ShapeDtypeStruct((NRHS, NRHS), jnp.float32),
        ],
        in_specs=[VMEM] * 4,
        out_specs=[VMEM] * 3,
        name="finish",
    )(parts, g, x, krylov)


def swap(value, blocks, rads, stride, parity):
    pairs = []
    for a in range(blocks):
        up = ((a // stride) + parity) % 2 == 0
        b = (a + stride if up else a - stride) % blocks
        pairs += [(a * rads + r, b * rads + r) for r in range(rads)]
    return lax.ppermute(value, ("ax", "rad"), pairs)


def gather(value, blocks, rads):
    out = [value]
    for m in range(1, rads):
        pairs = [(a * rads + r, a * rads + (r ^ m)) for a in range(blocks) for r in range(rads)]
        out.append(lax.ppermute(value, ("ax", "rad"), pairs))
    return out


def body(couplings, pivots, pattern, krylov):
    width = couplings.shape[3]
    blocks = lax.axis_size("ax")
    rads = lax.axis_size("rad")
    levels = blocks.bit_length() - 1
    block = lax.axis_index("ax")
    g = stored_gram(krylov)
    residue = krylov[0, krylov.shape[1] - NRHS :, :]
    slices = gather(residue, blocks, rads)
    weights = prep(0, 2, pattern, couplings, pattern)
    for rung in range(levels):
        stride = 1 << rung
        last = rung == levels - 1
        sent = level(1 if last else 2, slices, weights, g)
        if last:
            weights = prep_pivots(pivots, sent[0])
        else:
            weights = prep(rung + 1, 1 if rung + 2 == levels else 2, pattern, couplings, sent[0])
        got = swap(sent[0], blocks, rads, stride, 0)
        residue = residue - got[:NRHS]
        g = g + got[NRHS:, :128]
        if not last:
            other = swap(sent[1], blocks, rads, stride, 1)
            place = block // stride
            inside = jnp.where(place % 2 == 0, place > 0, place < blocks // stride - 1)
            residue = residue - jnp.where(inside, other, 0.0)
            slices = gather(residue, blocks, rads)
        else:
            tail = jnp.pad(g, ((0, 0), (0, residue.shape[1] - 128)))
            slices = gather(jnp.concatenate([residue, tail], axis=0), blocks, rads)
    x, part, g = solve(slices, weights, krylov)
    parts = lax.all_to_all(
        jnp.broadcast_to(part[None], (blocks * rads,) + part.shape), ("ax", "rad"), 0, 0
    )
    basis, coefficients, upper = finish(blocks * width, parts, g, x, krylov)
    return (basis, coefficients, upper)


def solution(mesh):
    return jax.shard_map(
        body,
        mesh=mesh,
        in_specs=(
            P("ax", None, "rad", None),
            P("ax", "rad", None),
            P("ax", None, None, None),
            P("ax", None, "rad"),
        ),
        out_specs=(P("ax", None, "rad"), P(), P()),
        check_vma=False,
    )
```

```python
import functools

import jax
import jax.numpy as jnp
from jax import lax
from jax.experimental import pallas as pl
from jax.experimental.pallas import tpu as pltpu
from jax.sharding import Mesh
from jax.sharding import PartitionSpec as P

NRHS = 16
GROUP = 48
precise = lax.Precision.HIGHEST


VMEM = pl.BlockSpec(memory_space=pltpu.VMEM)
SMEM = pl.BlockSpec(memory_space=pltpu.SMEM)
ANY = pl.BlockSpec(memory_space=pl.ANY)


def near(value):
    return pltpu.with_memory_space_constraint(value, pltpu.VMEM)


def far(value):
    return pltpu.with_memory_space_constraint(value, pltpu.HBM)


def made(shape, dtype=jnp.float32):
    return pltpu.VMEM(shape, dtype)


def nt_dot(a, b, precision=None):
    return lax.dot_general(
        a, b, (((1,), (1,)), ((), ())), precision=precision,
        preferred_element_type=jnp.float32,
    )


def nn_dot(a, b, precision=None):
    return lax.dot_general(
        a, b, (((1,), (0,)), ((), ())), precision=precision,
        preferred_element_type=jnp.float32,
    )


def split2(value):
    high = value.astype(jnp.bfloat16)
    low = (value - high.astype(jnp.float32)).astype(jnp.bfloat16)
    return high, low


def prep_kernel(rung, fields, slots, pattern_ref, couplings_ref, _, out_ref, keeps, sems):
    block = lax.axis_index(("chip", "core"))
    rad = lax.axis_index("rad")
    odd = (block // (1 << rung)) % 2
    rows, width = out_ref.shape[1:]
    points = width // fields
    cut = (rows // GROUP + 1) // 2 * GROUP
    kinds = [2 * rung + odd, 2 * rung + 1 - odd][:slots]
    copies = []
    for part, (start, size) in enumerate(((0, cut), (cut, rows - cut))):
        for slot, kind in enumerate(kinds):
            copy = pltpu.make_async_copy(
                couplings_ref.at[0, kind, pl.ds(start, size)],
                out_ref.at[slot, pl.ds(start, size)],
                sems.at[slot, part],
            )
            copy.start(priority=(slot + part) % 2 if slots == 1 else slot)
            copies.append((slot, start, size, copy))
    first = rad * rows // points
    col_field = lax.broadcasted_iota(jnp.int32, (8, width), 1) // points
    at_field = [col_field == col for col in range(fields)]
    for slot, kind in enumerate(kinds):
        for local in range(keeps.shape[1]):
            keep = jnp.zeros((8, width), jnp.float32)
            for col in range(fields):
                bit = pattern_ref[jnp.minimum(first + local, fields - 1), col, 0, kind]
                keep = jnp.where(at_field[col], bit.astype(jnp.float32), keep)
            keeps[slot, local] = jnp.concatenate([keep, keep], axis=0).astype(jnp.bfloat16)
    for slot, start, size, copy in copies:
        copy.wait()
        for group in range(start, start + size, GROUP):
            keep = keeps[slot, (rad * rows + group) // points - first]
            for tile in range(GROUP // 16):
                at = pl.ds(group + tile * 16, 16)
                out_ref[slot, at, :] = out_ref[slot, at, :] * keep


def prep(rung, slots, pattern, couplings, after):
    rows, width = couplings.shape[2:]
    fields = pattern.shape[0]
    spanned = rows // (width // fields) + 1
    return pl.pallas_call(
        functools.partial(prep_kernel, rung, fields, slots),
        out_shape=made((slots, rows, width), jnp.bfloat16),
        in_specs=[SMEM, ANY, ANY if rung == 0 else VMEM],
        out_specs=VMEM,
        scratch_shapes=[
            pltpu.VMEM((slots, spanned, 16, width), jnp.bfloat16),
            pltpu.SemaphoreType.DMA((slots, 2)),
        ],
        compiler_params=pltpu.CompilerParams(vmem_limit_bytes=4 << 20),
    )(pattern, far(couplings), after if rung == 0 else near(after))


def pivot_kernel(pivots_ref, _, out_ref, stage, sems):
    rows = pivots_ref.shape[1]
    part = rows // 3
    copies = []
    for i in range(3):
        copy = pltpu.make_async_copy(
            pivots_ref.at[0, pl.ds(i * part, part)], stage.at[pl.ds(i * part, part)], sems.at[i]
        )
        copy.start(priority=i % 2)
        copies.append(copy)
    for i, copy in enumerate(copies):
        copy.wait()
        for tile in range(part // 16):
            at = pl.ds(i * part + tile * 16, 16)
            high, low = split2(stage[at, :])
            out_ref[0, at, :] = high
            out_ref[1, at, :] = low


def prep_pivots(pivots, after):
    rows, width = pivots.shape[1:]
    return pl.pallas_call(
        pivot_kernel,
        out_shape=made((2, rows, width), jnp.bfloat16),
        in_specs=[ANY, VMEM],
        out_specs=VMEM,
        scratch_shapes=[pltpu.VMEM((rows, width), jnp.float32), pltpu.SemaphoreType.DMA((3,))],
        compiler_params=pltpu.CompilerParams(vmem_limit_bytes=8 << 20),
        name="prep_pivots",
    )(far(pivots), near(after))


def gather_rows(slices, whole):
    rad = lax.axis_index("rad")
    for m, piece in enumerate(slices):
        first = piece.shape[0] - NRHS if piece.shape[0] > NRHS + 8 else 0
        whole[rad ^ m] = piece[first : first + NRHS, :]
    v = jnp.concatenate([whole[t] for t in range(4)], axis=1)
    return jnp.concatenate(split2(v), axis=0)


def level_kernel(slots, s0, s1, s2, s3, w_ref, *rest):
    g_ref = rest[0] if len(rest) == slots + 2 else None
    outs, whole = rest[-slots - 1 : -1], rest[-1]
    if g_ref is None:
        stored = s0[...]
        product = nt_dot(stored, stored, precise)
        g = jnp.concatenate([product[8 * i : 8 * i + 8] for i in range(4)], axis=1)
    else:
        g = g_ref[...]
    lhs = gather_rows((s0, s1, s2, s3), whole)
    for slot in range(slots):
        both = nt_dot(lhs, w_ref[slot])
        outs[slot][:NRHS, :] = both[:NRHS] + both[NRHS:]
    outs[0][NRHS:, :128] = g
    outs[0][NRHS:, 128:] = jnp.zeros((8, outs[0].shape[1] - 128), jnp.float32)


def level(slots, slices, weights, g):
    rows = weights.shape[1]
    args = (*slices, weights) if g is None else (*slices, weights, g)
    shapes = [(NRHS + 8, rows), (NRHS, rows)][:slots]
    return pl.pallas_call(
        functools.partial(level_kernel, slots),
        out_shape=[made(s) for s in shapes],
        in_specs=[VMEM] * len(args),
        out_specs=[VMEM] * slots,
        scratch_shapes=[pltpu.VMEM((4, NRHS, rows), jnp.float32)],
        compiler_params=pltpu.CompilerParams(vmem_limit_bytes=4 << 20),
        name="level",
    )(*map(near, args))


def solve_kernel(s0, s1, s2, s3, p_ref, stored_ref, x_ref, part_ref, g_ref, whole, gs):
    rad = lax.axis_index("rad")
    lhs = gather_rows((s0, s1, s2, s3), whole)
    both = nt_dot(lhs, p_ref[0])
    x = both[:NRHS] + both[NRHS:] + nt_dot(lhs[:NRHS], p_ref[1])
    x_ref[...] = x
    t = jnp.concatenate(
        [nt_dot(x, stored_ref[0], precise), nt_dot(x, x, precise)], axis=1
    )
    part_ref[...] = jnp.concatenate(
        [t[:8], t[8:], jnp.zeros((8, 32), jnp.float32)], axis=1
    )
    for m, piece in enumerate((s0, s1, s2, s3)):
        gs[rad ^ m] = piece[NRHS:, :128]
    g_ref[...] = (gs[0] + gs[1]) + (gs[2] + gs[3])


def solve(slices, pivots, krylov):
    rows = pivots.shape[1]
    return pl.pallas_call(
        solve_kernel,
        out_shape=[
            made((NRHS, rows)),
            made((8, 128)),
            made((8, 128)),
        ],
        in_specs=[VMEM] * 6,
        out_specs=[VMEM] * 3,
        scratch_shapes=[
            pltpu.VMEM((4, NRHS, rows), jnp.float32),
            pltpu.VMEM((4, 8, 128), jnp.float32),
        ],
        compiler_params=pltpu.CompilerParams(vmem_limit_bytes=8 << 20),
        name="solve",
    )(*map(near, (*slices, pivots, krylov)))


def finish_kernel(total, parts_ref, g_ref, x_ref, stored_ref, basis_ref, coef_ref, upper_ref):
    s = jnp.sum(parts_ref[...], axis=0) * (1.0 / total)
    t = jnp.concatenate([s[:, :48], s[:, 48:96]], axis=0)
    gs = g_ref[...] * (1.0 / total)
    g = jnp.concatenate([gs[:, 32 * i : 32 * i + 32] for i in range(4)], axis=0)
    ct = t[:, :32]
    xx = t[:, 32:48]
    coef_ref[...] = ct
    stored = stored_ref[0]
    remainder = x_ref[...] - nn_dot(ct, stored, precise)
    gram = xx - nt_dot(2.0 * ct - nn_dot(ct, g, precise), ct, precise)
    row = lax.broadcasted_iota(jnp.int32, (NRHS, 2 * NRHS), 0)
    col = lax.broadcasted_iota(jnp.int32, (NRHS, 2 * NRHS), 1)
    eye = (lax.broadcasted_iota(jnp.int32, (NRHS, NRHS), 0)
           == lax.broadcasted_iota(jnp.int32, (NRHS, NRHS), 1)).astype(jnp.float32)
    a = jnp.concatenate([gram, eye], axis=1)
    for k in range(NRHS - 1):
        factor = a[:, k : k + 1] / a[k : k + 1, k : k + 1]
        a = jnp.where(row > k, a - factor * a[k : k + 1, :], a)
    diag = jnp.sum(jnp.where(row == col, a, 0.0), axis=1, keepdims=True)
    a = a * lax.rsqrt(diag)
    u = a[:, :NRHS]
    upper_ref[...] = jnp.where(row[:, :NRHS] <= col[:, :NRHS], u, 0.0)
    basis_ref[0] = nn_dot(a[:, NRHS:], remainder, precise)


def finish(total, parts, g, x, krylov):
    rows = x.shape[1]
    stored = krylov.shape[1]
    return pl.pallas_call(
        functools.partial(finish_kernel, total),
        out_shape=[
            jax.ShapeDtypeStruct((1, NRHS, rows), jnp.float32),
            jax.ShapeDtypeStruct((NRHS, stored), jnp.float32),
            jax.ShapeDtypeStruct((NRHS, NRHS), jnp.float32),
        ],
        in_specs=[VMEM] * 4,
        out_specs=[VMEM] * 3,
        compiler_params=pltpu.CompilerParams(vmem_limit_bytes=8 << 20),
        name="finish",
    )(*map(near, (parts, g, x, krylov)))


ALL = ("chip", "core", "rad")


def swap(value, blocks, rads, stride, parity):
    pairs = []
    for a in range(blocks):
        up = ((a // stride) + parity) % 2 == 0
        b = (a + stride if up else a - stride) % blocks
        pairs += [(a * rads + r, b * rads + r) for r in range(rads)]
    return lax.ppermute(value, ALL, pairs)


def gather(value, blocks, rads):
    out = [value]
    for m in range(1, rads):
        pairs = [(a * rads + r, a * rads + (r ^ m)) for a in range(blocks) for r in range(rads)]
        out.append(lax.ppermute(value, ALL, pairs))
    return out


def step(couplings, pivots, pattern, krylov):
    width = couplings.shape[3]
    blocks = lax.axis_size("chip") * lax.axis_size("core")
    rads = lax.axis_size("rad")
    levels = blocks.bit_length() - 1
    block = lax.axis_index(("chip", "core"))
    pattern = pattern.transpose(2, 3, 0, 1)
    slices = gather(krylov[0], blocks, rads)
    weights = prep(0, 2, pattern, couplings, krylov)
    g = None
    residue = krylov[0, krylov.shape[1] - NRHS :, :]
    for rung in range(levels):
        stride = 1 << rung
        last = rung == levels - 1
        sent = level(1 if last else 2, slices, weights, g)
        if last:
            weights = prep_pivots(pivots, sent[0])
        else:
            weights = prep(rung + 1, 1 if rung + 2 == levels else 2, pattern, couplings, sent[0])
        got = swap(sent[0], blocks, rads, stride, 0)
        other = None if last else swap(sent[1], blocks, rads, stride, 1)
        residue = residue - got[:NRHS]
        g = (sent[0][NRHS:, :128] if g is None else g) + got[NRHS:, :128]
        if not last:
            place = block // stride
            inside = jnp.where(place % 2 == 0, place > 0, place < blocks // stride - 1)
            residue = residue - jnp.where(inside, other, 0.0)
            payload = residue
        else:
            tail = jnp.pad(g, ((0, 0), (0, residue.shape[1] - 128)))
            payload = jnp.concatenate([residue, tail], axis=0)
        slices = gather(payload, blocks, rads)
    x, part, g = solve(slices, weights, krylov)
    part = part + swap(part, blocks, rads, 1, 0)
    chips = blocks // 2 * rads
    parts = lax.all_to_all(
        jnp.broadcast_to(part[None], (chips,) + part.shape), ("chip", "rad"), 0, 0
    )
    basis, coefficients, upper = finish(blocks * width, parts, g, x, krylov)
    return (basis, coefficients.T, upper)


def solution(mesh):
    blocks, rads = mesh.shape["ax"], mesh.shape["rad"]
    split = Mesh(mesh.devices.reshape(blocks // 2, 2, rads), ALL)
    ax = ("chip", "core")
    return jax.shard_map(
        step,
        mesh=split,
        in_specs=(
            P(ax, None, "rad", None),
            P(ax, "rad", None),
            P(ax, None, None, None),
            P(ax, None, "rad"),
        ),
        out_specs=(P(ax, None, "rad"), P(), P()),
        check_vma=False,
    )
```

```python
import functools

import jax
import jax.numpy as jnp
from jax import lax
from jax.experimental import pallas as pl
from jax.experimental.pallas import tpu as pltpu
from jax.sharding import Mesh
from jax.sharding import PartitionSpec as P

NRHS = 16
precise = lax.Precision.HIGHEST


VMEM = pl.BlockSpec(memory_space=pltpu.VMEM)
SMEM = pl.BlockSpec(memory_space=pltpu.SMEM)
ANY = pl.BlockSpec(memory_space=pl.ANY)


def near(value):
    return pltpu.with_memory_space_constraint(value, pltpu.VMEM)


def far(value):
    return pltpu.with_memory_space_constraint(value, pltpu.HBM)


def made(shape, dtype=jnp.float32):
    return pltpu.VMEM(shape, dtype)


def nt_dot(a, b, precision=None):
    return lax.dot_general(
        a, b, (((1,), (1,)), ((), ())), precision=precision,
        preferred_element_type=jnp.float32,
    )


def nn_dot(a, b, precision=None):
    return lax.dot_general(
        a, b, (((1,), (0,)), ((), ())), precision=precision,
        preferred_element_type=jnp.float32,
    )


def split2(value):
    high = value.astype(jnp.bfloat16)
    low = (value - high.astype(jnp.float32)).astype(jnp.bfloat16)
    return high, low


def masks_kernel(pattern_ref, out_ref):
    spanned, kinds_pad, width = out_ref.shape
    fields, _, _, kinds = pattern_ref.shape
    points = width // fields
    first = lax.axis_index("rad") * (width // lax.axis_size("rad")) // points
    col_field = lax.broadcasted_iota(jnp.int32, (kinds_pad, width), 1) // points
    for local in range(spanned):
        field = jnp.minimum(first + local, fields - 1)
        rows = [pattern_ref[field, col, :, :].astype(jnp.float32) for col in range(fields)]
        table = jnp.concatenate(rows, axis=0)
        table = jnp.concatenate(
            [table, jnp.zeros((fields, 128 - kinds), jnp.float32)], axis=1
        )
        table = jnp.concatenate([table, jnp.zeros((16 - fields, 128), jnp.float32)], axis=0)
        by_kind = table.T[:kinds_pad]
        keep = jnp.zeros((kinds_pad, width), jnp.float32)
        for col in range(fields):
            keep = jnp.where(col_field == col, by_kind[:, col : col + 1], keep)
        out_ref[local] = keep


def make_masks(pattern, rows, width):
    fields, _, _, _ = pattern.shape
    spanned = rows // (width // fields) + 1
    return pl.pallas_call(
        masks_kernel,
        out_shape=made((spanned, 16, width)),
        in_specs=[VMEM],
        out_specs=VMEM,
        compiler_params=pltpu.CompilerParams(vmem_limit_bytes=4 << 20),
        name="masks",
    )(near(pattern))


def kind_of(rung, slot):
    odd = (lax.axis_index(("chip", "core")) // (1 << rung)) % 2
    return 2 * rung + (odd if slot == 0 else 1 - odd)


def fetch_kernel(rung, slots, couplings_ref, *rest):
    out_ref, sems = rest[-2:]
    copies = []
    for slot in range(slots):
        copy = pltpu.make_async_copy(
            couplings_ref.at[0, kind_of(rung, slot)], out_ref.at[slot], sems.at[slot]
        )
        copy.start(priority=slot)
        copies.append(copy)
    for copy in copies:
        copy.wait()


def fetch(rung, slots, couplings, after=None):
    rows, width = couplings.shape[2:]
    args = (far(couplings),) if after is None else (far(couplings), near(after))
    return pl.pallas_call(
        functools.partial(fetch_kernel, rung, slots),
        out_shape=made((slots, rows, width), jnp.bfloat16),
        in_specs=[ANY, VMEM][: len(args)],
        out_specs=VMEM,
        scratch_shapes=[pltpu.SemaphoreType.DMA((slots,))],
        compiler_params=pltpu.CompilerParams(vmem_limit_bytes=4 << 20),
    )(*args)


def pivot_kernel(pivots_ref, _, out_ref, stage, sems):
    rows = pivots_ref.shape[1]
    part = rows // 3
    copies = []
    for i in range(3):
        copy = pltpu.make_async_copy(
            pivots_ref.at[0, pl.ds(i * part, part)], stage.at[pl.ds(i * part, part)], sems.at[i]
        )
        copy.start(priority=i % 2)
        copies.append(copy)
    for i, copy in enumerate(copies):
        copy.wait()
        for tile in range(part // 16):
            at = pl.ds(i * part + tile * 16, 16)
            high, low = split2(stage[at, :])
            out_ref[0, at, :] = high
            out_ref[1, at, :] = low


def prep_pivots(pivots, after):
    rows, width = pivots.shape[1:]
    return pl.pallas_call(
        pivot_kernel,
        out_shape=made((2, rows, width), jnp.bfloat16),
        in_specs=[ANY, VMEM],
        out_specs=VMEM,
        scratch_shapes=[pltpu.VMEM((rows, width), jnp.float32), pltpu.SemaphoreType.DMA((3,))],
        compiler_params=pltpu.CompilerParams(vmem_limit_bytes=8 << 20),
        name="prep_pivots",
    )(far(pivots), near(after))


def gather_rows(slices, whole):
    rad = lax.axis_index("rad")
    for m, piece in enumerate(slices):
        first = piece.shape[0] - NRHS if piece.shape[0] > NRHS + 8 else 0
        whole[rad ^ m] = piece[first : first + NRHS, :]
    v = jnp.concatenate([whole[t] for t in range(4)], axis=1)
    return jnp.concatenate(split2(v), axis=0)


def level_kernel(rung, slots, points, s0, s1, s2, s3, w_ref, masks_ref, *rest):
    g_ref = rest[0] if len(rest) == slots + 2 else None
    outs, whole = rest[-slots - 1 : -1], rest[-1]
    if g_ref is None:
        stored = s0[...]
        product = nt_dot(stored, stored, precise)
        g = jnp.concatenate([product[8 * i : 8 * i + 8] for i in range(4)], axis=1)
    else:
        g = g_ref[...]
    lhs = gather_rows((s0, s1, s2, s3), whole)
    spanned = masks_ref.shape[0]
    rows = w_ref.shape[1]
    offset = lax.axis_index("rad") * rows
    first = offset // points
    row = offset + lax.broadcasted_iota(jnp.int32, (NRHS, rows), 1)
    for slot in range(slots):
        kind = kind_of(rung, slot)
        parts = []
        for local in range(spanned):
            keep = masks_ref[local, pl.ds(kind, 1), :]
            keep = jnp.broadcast_to(keep, (16, keep.shape[1])).astype(jnp.bfloat16)
            parts.append(lhs * jnp.concatenate([keep, keep], axis=0))
        product = nt_dot(jnp.concatenate(parts, axis=0), w_ref[slot])
        push = None
        for local in reversed(range(spanned)):
            at = 2 * NRHS * local
            one = product[at : at + NRHS] + product[at + NRHS : at + 2 * NRHS]
            push = one if push is None else jnp.where(row < (first + local + 1) * points, one, push)
        outs[slot][:NRHS, :] = push
    outs[0][NRHS:, :128] = g
    outs[0][NRHS:, 128:] = jnp.zeros((8, outs[0].shape[1] - 128), jnp.float32)


def level(rung, slots, points, slices, weights, masks, g):
    rows = weights.shape[1]
    args = (*slices, weights, masks) if g is None else (*slices, weights, masks, g)
    shapes = [(NRHS + 8, rows), (NRHS, rows)][:slots]
    return pl.pallas_call(
        functools.partial(level_kernel, rung, slots, points),
        out_shape=[made(s) for s in shapes],
        in_specs=[VMEM] * len(args),
        out_specs=[VMEM] * slots,
        scratch_shapes=[pltpu.VMEM((4, NRHS, rows), jnp.float32)],
        compiler_params=pltpu.CompilerParams(vmem_limit_bytes=4 << 20),
        name="level",
    )(*map(near, args))


def solve_kernel(s0, s1, s2, s3, p_ref, stored_ref, x_ref, part_ref, g_ref, whole, gs):
    rad = lax.axis_index("rad")
    lhs = gather_rows((s0, s1, s2, s3), whole)
    both = nt_dot(lhs, p_ref[0])
    x = both[:NRHS] + both[NRHS:] + nt_dot(lhs[:NRHS], p_ref[1])
    x_ref[...] = x
    t = jnp.concatenate(
        [nt_dot(x, stored_ref[0], precise), nt_dot(x, x, precise)], axis=1
    )
    part_ref[...] = jnp.concatenate(
        [t[:8], t[8:], jnp.zeros((8, 32), jnp.float32)], axis=1
    )
    for m, piece in enumerate((s0, s1, s2, s3)):
        gs[rad ^ m] = piece[NRHS:, :128]
    g_ref[...] = (gs[0] + gs[1]) + (gs[2] + gs[3])


def solve(slices, pivots, krylov):
    rows = pivots.shape[1]
    return pl.pallas_call(
        solve_kernel,
        out_shape=[
            made((NRHS, rows)),
            made((8, 128)),
            made((8, 128)),
        ],
        in_specs=[VMEM] * 6,
        out_specs=[VMEM] * 3,
        scratch_shapes=[
            pltpu.VMEM((4, NRHS, rows), jnp.float32),
            pltpu.VMEM((4, 8, 128), jnp.float32),
        ],
        compiler_params=pltpu.CompilerParams(vmem_limit_bytes=8 << 20),
        name="solve",
    )(*map(near, (*slices, pivots, krylov)))


def finish_kernel(total, parts_ref, g_ref, x_ref, stored_ref, basis_ref, coef_ref, upper_ref):
    s = jnp.sum(parts_ref[...], axis=0) * (1.0 / total)
    t = jnp.concatenate([s[:, :48], s[:, 48:96]], axis=0)
    gs = g_ref[...] * (1.0 / total)
    g = jnp.concatenate([gs[:, 32 * i : 32 * i + 32] for i in range(4)], axis=0)
    ct = t[:, :32]
    xx = t[:, 32:48]
    coef_ref[...] = ct
    stored = stored_ref[0]
    remainder = x_ref[...] - nn_dot(ct, stored, precise)
    gram = xx - nt_dot(2.0 * ct - nn_dot(ct, g, precise), ct, precise)
    row = lax.broadcasted_iota(jnp.int32, (NRHS, 2 * NRHS), 0)
    col = lax.broadcasted_iota(jnp.int32, (NRHS, 2 * NRHS), 1)
    eye = (lax.broadcasted_iota(jnp.int32, (NRHS, NRHS), 0)
           == lax.broadcasted_iota(jnp.int32, (NRHS, NRHS), 1)).astype(jnp.float32)
    a = jnp.concatenate([gram, eye], axis=1)
    for k in range(NRHS - 1):
        factor = a[:, k : k + 1] / a[k : k + 1, k : k + 1]
        a = jnp.where(row > k, a - factor * a[k : k + 1, :], a)
    diag = jnp.sum(jnp.where(row == col, a, 0.0), axis=1, keepdims=True)
    a = a * lax.rsqrt(diag)
    u = a[:, :NRHS]
    upper_ref[...] = jnp.where(row[:, :NRHS] <= col[:, :NRHS], u, 0.0)
    basis_ref[0] = nn_dot(a[:, NRHS:], remainder, precise)


def finish(total, parts, g, x, krylov):
    rows = x.shape[1]
    stored = krylov.shape[1]
    return pl.pallas_call(
        functools.partial(finish_kernel, total),
        out_shape=[
            jax.ShapeDtypeStruct((1, NRHS, rows), jnp.float32),
            jax.ShapeDtypeStruct((NRHS, stored), jnp.float32),
            jax.ShapeDtypeStruct((NRHS, NRHS), jnp.float32),
        ],
        in_specs=[VMEM] * 4,
        out_specs=[VMEM] * 3,
        compiler_params=pltpu.CompilerParams(vmem_limit_bytes=8 << 20),
        name="finish",
    )(*map(near, (parts, g, x, krylov)))


ALL = ("chip", "core", "rad")


def swap(value, blocks, rads, stride, parity):
    pairs = []
    for a in range(blocks):
        up = ((a // stride) + parity) % 2 == 0
        b = (a + stride if up else a - stride) % blocks
        pairs += [(a * rads + r, b * rads + r) for r in range(rads)]
    return lax.ppermute(value, ALL, pairs)


def gather(value, blocks, rads):
    out = [value]
    for m in range(1, rads):
        pairs = [(a * rads + r, a * rads + (r ^ m)) for a in range(blocks) for r in range(rads)]
        out.append(lax.ppermute(value, ALL, pairs))
    return out


def step(couplings, pivots, pattern, krylov):
    width = couplings.shape[3]
    blocks = lax.axis_size("chip") * lax.axis_size("core")
    rads = lax.axis_size("rad")
    levels = blocks.bit_length() - 1
    block = lax.axis_index(("chip", "core"))
    pattern = pattern.transpose(2, 3, 0, 1)
    slices = gather(krylov[0], blocks, rads)
    weights = fetch(0, 2, couplings)
    masks = make_masks(pattern, couplings.shape[2], width)
    points = width // pattern.shape[0]
    g = None
    residue = krylov[0, krylov.shape[1] - NRHS :, :]
    for rung in range(levels):
        stride = 1 << rung
        last = rung == levels - 1
        sent = level(rung, 1 if last else 2, points, slices, weights, masks, g)
        if last:
            weights = prep_pivots(pivots, sent[0])
        else:
            weights = fetch(rung + 1, 1 if rung + 2 == levels else 2, couplings, sent[0])
        got = swap(sent[0], blocks, rads, stride, 0)
        other = None if last else swap(sent[1], blocks, rads, stride, 1)
        residue = residue - got[:NRHS]
        g = (sent[0][NRHS:, :128] if g is None else g) + got[NRHS:, :128]
        if not last:
            place = block // stride
            inside = jnp.where(place % 2 == 0, place > 0, place < blocks // stride - 1)
            residue = residue - jnp.where(inside, other, 0.0)
            payload = residue
        else:
            tail = jnp.pad(g, ((0, 0), (0, residue.shape[1] - 128)))
            payload = jnp.concatenate([residue, tail], axis=0)
        slices = gather(payload, blocks, rads)
    x, part, g = solve(slices, weights, krylov)
    part = part + swap(part, blocks, rads, 1, 0)
    chips = blocks // 2 * rads
    parts = lax.all_to_all(
        jnp.broadcast_to(part[None], (chips,) + part.shape), ("chip", "rad"), 0, 0
    )
    basis, coefficients, upper = finish(blocks * width, parts, g, x, krylov)
    return (basis, coefficients.T, upper)


def solution(mesh):
    blocks, rads = mesh.shape["ax"], mesh.shape["rad"]
    split = Mesh(mesh.devices.reshape(blocks // 2, 2, rads), ALL)
    ax = ("chip", "core")
    return jax.shard_map(
        step,
        mesh=split,
        in_specs=(
            P(ax, None, "rad", None),
            P(ax, "rad", None),
            P(ax, None, None, None),
            P(ax, None, "rad"),
        ),
        out_specs=(P(ax, None, "rad"), P(), P()),
        check_vma=False,
    )
```

```python
import functools

import jax
import jax.numpy as jnp
from jax import lax
from jax.experimental import pallas as pl
from jax.experimental.pallas import tpu as pltpu
from jax.sharding import Mesh
from jax.sharding import PartitionSpec as P

NRHS = 16
precise = lax.Precision.HIGHEST


VMEM = pl.BlockSpec(memory_space=pltpu.VMEM)
SMEM = pl.BlockSpec(memory_space=pltpu.SMEM)
ANY = pl.BlockSpec(memory_space=pl.ANY)


def near(value):
    return pltpu.with_memory_space_constraint(value, pltpu.VMEM)


def far(value):
    return pltpu.with_memory_space_constraint(value, pltpu.HBM)


def made(shape, dtype=jnp.float32):
    return pltpu.VMEM(shape, dtype)


def nt_dot(a, b, precision=None):
    return lax.dot_general(
        a, b, (((1,), (1,)), ((), ())), precision=precision,
        preferred_element_type=jnp.float32,
    )


def nn_dot(a, b, precision=None):
    return lax.dot_general(
        a, b, (((1,), (0,)), ((), ())), precision=precision,
        preferred_element_type=jnp.float32,
    )


def split2(value):
    high = value.astype(jnp.bfloat16)
    low = (value - high.astype(jnp.float32)).astype(jnp.bfloat16)
    return high, low


def masks_kernel(pattern_ref, out_ref):
    spanned, kinds_pad, width = out_ref.shape
    fields, _, _, kinds = pattern_ref.shape
    points = width // fields
    first = lax.axis_index("rad") * (width // lax.axis_size("rad")) // points
    col_field = lax.broadcasted_iota(jnp.int32, (kinds_pad, width), 1) // points
    for local in range(spanned):
        field = jnp.minimum(first + local, fields - 1)
        rows = [pattern_ref[field, col, :, :].astype(jnp.float32) for col in range(fields)]
        table = jnp.concatenate(rows, axis=0)
        table = jnp.concatenate(
            [table, jnp.zeros((fields, 128 - kinds), jnp.float32)], axis=1
        )
        table = jnp.concatenate([table, jnp.zeros((16 - fields, 128), jnp.float32)], axis=0)
        by_kind = table.T[:kinds_pad]
        keep = jnp.zeros((kinds_pad, width), jnp.float32)
        for col in range(fields):
            keep = jnp.where(col_field == col, by_kind[:, col : col + 1], keep)
        out_ref[local] = keep


def make_masks(pattern, rows, width):
    fields, _, _, _ = pattern.shape
    spanned = rows // (width // fields) + 1
    return pl.pallas_call(
        masks_kernel,
        out_shape=made((spanned, 16, width)),
        in_specs=[VMEM],
        out_specs=VMEM,
        compiler_params=pltpu.CompilerParams(vmem_limit_bytes=4 << 20),
        name="masks",
    )(near(pattern))


def kind_of(rung, slot):
    odd = (lax.axis_index(("chip", "core")) // (1 << rung)) % 2
    return 2 * rung + (odd if slot == 0 else 1 - odd)


def fetch_kernel(rung, slots, couplings_ref, *rest):
    out_ref, sems = rest[-2:]
    copies = []
    for slot in range(slots):
        copy = pltpu.make_async_copy(
            couplings_ref.at[0, kind_of(rung, slot)], out_ref.at[slot], sems.at[slot]
        )
        copy.start(priority=slot)
        copies.append(copy)
    for copy in copies:
        copy.wait()


def fetch(rung, slots, couplings, after=None):
    rows, width = couplings.shape[2:]
    args = (far(couplings),) if after is None else (far(couplings), near(after))
    return pl.pallas_call(
        functools.partial(fetch_kernel, rung, slots),
        out_shape=made((slots, rows, width), jnp.bfloat16),
        in_specs=[ANY, VMEM][: len(args)],
        out_specs=VMEM,
        scratch_shapes=[pltpu.SemaphoreType.DMA((slots,))],
        compiler_params=pltpu.CompilerParams(vmem_limit_bytes=4 << 20),
    )(*args)


def pivot_kernel(pivots_ref, _, out_ref, stage, sems):
    rows = pivots_ref.shape[1]
    part = rows // 3
    copies = []
    for i in range(3):
        copy = pltpu.make_async_copy(
            pivots_ref.at[0, pl.ds(i * part, part)], stage.at[pl.ds(i * part, part)], sems.at[i]
        )
        copy.start(priority=i % 2)
        copies.append(copy)
    for i, copy in enumerate(copies):
        copy.wait()
        for tile in range(part // 16):
            at = pl.ds(i * part + tile * 16, 16)
            high, low = split2(stage[at, :])
            out_ref[0, at, :] = high
            out_ref[1, at, :] = low


def prep_pivots(pivots, after):
    rows, width = pivots.shape[1:]
    return pl.pallas_call(
        pivot_kernel,
        out_shape=made((2, rows, width), jnp.bfloat16),
        in_specs=[ANY, VMEM],
        out_specs=VMEM,
        scratch_shapes=[pltpu.VMEM((rows, width), jnp.float32), pltpu.SemaphoreType.DMA((3,))],
        compiler_params=pltpu.CompilerParams(vmem_limit_bytes=8 << 20),
        name="prep_pivots",
    )(far(pivots), near(after))


def gather_rows(slices, whole):
    rad = lax.axis_index("rad")
    for m, piece in enumerate(slices):
        first = piece.shape[0] - NRHS if piece.shape[0] > NRHS + 8 else 0
        whole[rad ^ m] = piece[first : first + NRHS, :]
    v = jnp.concatenate([whole[t] for t in range(4)], axis=1)
    return jnp.concatenate(split2(v), axis=0)


def level_kernel(rung, slots, points, s0, s1, s2, s3, w_ref, masks_ref, *rest):
    g_ref = rest[0] if len(rest) == slots + 2 else None
    outs, whole = rest[-slots - 1 : -1], rest[-1]
    if g_ref is None:
        stored = s0[...]
        product = nt_dot(stored, stored, precise)
        g = jnp.concatenate([product[8 * i : 8 * i + 8] for i in range(4)], axis=1)
    else:
        g = g_ref[...]
    lhs = gather_rows((s0, s1, s2, s3), whole)
    spanned = masks_ref.shape[0]
    rows = w_ref.shape[1]
    offset = lax.axis_index("rad") * rows
    first = offset // points
    row = offset + lax.broadcasted_iota(jnp.int32, (NRHS, rows), 1)
    for slot in range(slots):
        kind = kind_of(rung, slot)
        parts = []
        for local in range(spanned):
            keep = masks_ref[local, pl.ds(kind, 1), :]
            keep = jnp.broadcast_to(keep, (16, keep.shape[1])).astype(jnp.bfloat16)
            parts.append(lhs * jnp.concatenate([keep, keep], axis=0))
        product = nt_dot(jnp.concatenate(parts, axis=0), w_ref[slot])
        push = None
        for local in reversed(range(spanned)):
            at = 2 * NRHS * local
            one = product[at : at + NRHS] + product[at + NRHS : at + 2 * NRHS]
            push = one if push is None else jnp.where(row < (first + local + 1) * points, one, push)
        outs[slot][:NRHS, :] = push
    outs[0][NRHS:, :128] = g
    outs[0][NRHS:, 128:] = jnp.zeros((8, outs[0].shape[1] - 128), jnp.float32)


def level(rung, slots, points, slices, weights, masks, g):
    rows = weights.shape[1]
    args = (*slices, weights, masks) if g is None else (*slices, weights, masks, g)
    shapes = [(NRHS + 8, rows), (NRHS, rows)][:slots]
    return pl.pallas_call(
        functools.partial(level_kernel, rung, slots, points),
        out_shape=[made(s) for s in shapes],
        in_specs=[VMEM] * len(args),
        out_specs=[VMEM] * slots,
        scratch_shapes=[pltpu.VMEM((4, NRHS, rows), jnp.float32)],
        compiler_params=pltpu.CompilerParams(vmem_limit_bytes=4 << 20),
        name="level",
    )(*map(near, args))


def solve_kernel(s0, s1, s2, s3, p_ref, stored_ref, x_ref, part_ref, g_ref, whole, gs):
    rad = lax.axis_index("rad")
    lhs = gather_rows((s0, s1, s2, s3), whole)
    both = nt_dot(lhs, p_ref[0])
    x = both[:NRHS] + both[NRHS:] + nt_dot(lhs[:NRHS], p_ref[1])
    x_ref[...] = x
    t = jnp.concatenate(
        [nt_dot(x, stored_ref[0], precise), nt_dot(x, x, precise)], axis=1
    )
    part_ref[...] = jnp.concatenate(
        [t[:8], t[8:], jnp.zeros((8, 32), jnp.float32)], axis=1
    )
    for m, piece in enumerate((s0, s1, s2, s3)):
        gs[rad ^ m] = piece[NRHS:, :128]
    g_ref[...] = (gs[0] + gs[1]) + (gs[2] + gs[3])


def solve(slices, pivots, krylov):
    rows = pivots.shape[1]
    return pl.pallas_call(
        solve_kernel,
        out_shape=[
            made((NRHS, rows)),
            made((8, 128)),
            made((8, 128)),
        ],
        in_specs=[VMEM] * 6,
        out_specs=[VMEM] * 3,
        scratch_shapes=[
            pltpu.VMEM((4, NRHS, rows), jnp.float32),
            pltpu.VMEM((4, 8, 128), jnp.float32),
        ],
        compiler_params=pltpu.CompilerParams(vmem_limit_bytes=8 << 20),
        name="solve",
    )(*map(near, (*slices, pivots, krylov)))


def finish_kernel(total, parts_ref, g_ref, x_ref, stored_ref, basis_ref, coef_ref, upper_ref):
    s = jnp.sum(parts_ref[...], axis=0) * (1.0 / total)
    t = jnp.concatenate([s[:, :48], s[:, 48:96]], axis=0)
    gs = g_ref[...] * (1.0 / total)
    g = jnp.concatenate([gs[:, 32 * i : 32 * i + 32] for i in range(4)], axis=0)
    ct = t[:, :32]
    xx = t[:, 32:48]
    coef_ref[...] = ct
    stored = stored_ref[0]
    remainder = x_ref[...] - nn_dot(ct, stored, precise)
    gram = xx - nt_dot(2.0 * ct - nn_dot(ct, g, precise), ct, precise)
    sub = lax.broadcasted_iota(jnp.int32, (NRHS, 128), 0)
    lane = lax.broadcasted_iota(jnp.int32, (NRHS, 128), 1)
    rows = [jnp.broadcast_to(gram[:, i : i + 1], (NRHS, 128)) for i in range(NRHS)]
    for k in range(NRHS - 1):
        inverse = 1.0 / rows[k][k : k + 1, :]
        at_pivot = sub == k
        pivot_row = jnp.where(at_pivot, 1.0, rows[k])
        for i in range(k + 1, NRHS):
            factor = rows[i][k : k + 1, :] * inverse
            rows[i] = jnp.where(at_pivot, 0.0, rows[i]) - factor * pivot_row
    packed = rows[0]
    for i in range(1, NRHS):
        packed = jnp.where(lane == i, rows[i], packed)
    on_diag = sub == lane
    diag = jnp.sum(jnp.where(on_diag, packed, 0.0), axis=0, keepdims=True)
    scale = lax.rsqrt(jnp.where(lane[:1] < NRHS, diag, 1.0))
    lower = jnp.where(sub >= lane, packed, 0.0) * scale
    inverse_t = jnp.where(on_diag, 1.0, jnp.where(sub < lane, packed, 0.0)) * scale
    upper_ref[...] = lower.T[:NRHS, :]
    basis_ref[0] = nn_dot(inverse_t.T[:NRHS, :], remainder, precise)


def finish(total, parts, g, x, krylov):
    rows = x.shape[1]
    stored = krylov.shape[1]
    return pl.pallas_call(
        functools.partial(finish_kernel, total),
        out_shape=[
            jax.ShapeDtypeStruct((1, NRHS, rows), jnp.float32),
            jax.ShapeDtypeStruct((NRHS, stored), jnp.float32),
            jax.ShapeDtypeStruct((NRHS, NRHS), jnp.float32),
        ],
        in_specs=[VMEM] * 4,
        out_specs=[VMEM] * 3,
        compiler_params=pltpu.CompilerParams(vmem_limit_bytes=8 << 20),
        name="finish",
    )(*map(near, (parts, g, x, krylov)))


ALL = ("chip", "core", "rad")


def swap(value, blocks, rads, stride, parity):
    pairs = []
    for a in range(blocks):
        up = ((a // stride) + parity) % 2 == 0
        b = (a + stride if up else a - stride) % blocks
        pairs += [(a * rads + r, b * rads + r) for r in range(rads)]
    return lax.ppermute(value, ALL, pairs)


def gather(value, blocks, rads):
    out = [value]
    for m in range(1, rads):
        pairs = [(a * rads + r, a * rads + (r ^ m)) for a in range(blocks) for r in range(rads)]
        out.append(lax.ppermute(value, ALL, pairs))
    return out


def step(couplings, pivots, pattern, krylov):
    width = couplings.shape[3]
    blocks = lax.axis_size("chip") * lax.axis_size("core")
    rads = lax.axis_size("rad")
    levels = blocks.bit_length() - 1
    block = lax.axis_index(("chip", "core"))
    pattern = pattern.transpose(2, 3, 0, 1)
    slices = gather(krylov[0], blocks, rads)
    weights = fetch(0, 2, couplings)
    masks = make_masks(pattern, couplings.shape[2], width)
    points = width // pattern.shape[0]
    g = None
    residue = krylov[0, krylov.shape[1] - NRHS :, :]
    for rung in range(levels):
        stride = 1 << rung
        last = rung == levels - 1
        sent = level(rung, 1 if last else 2, points, slices, weights, masks, g)
        got = swap(sent[0], blocks, rads, stride, 0)
        other = None if last else swap(sent[1], blocks, rads, stride, 1)
        residue = residue - got[:NRHS]
        g = (sent[0][NRHS:, :128] if g is None else g) + got[NRHS:, :128]
        if not last:
            place = block // stride
            inside = jnp.where(place % 2 == 0, place > 0, place < blocks // stride - 1)
            residue = residue - jnp.where(inside, other, 0.0)
            payload = residue
        else:
            tail = jnp.pad(g, ((0, 0), (0, residue.shape[1] - 128)))
            payload = jnp.concatenate([residue, tail], axis=0)
        slices = gather(payload, blocks, rads)
        if last:
            weights = prep_pivots(pivots, payload)
        else:
            weights = fetch(rung + 1, 1 if rung + 2 == levels else 2, couplings, payload)
    x, part, g = solve(slices, weights, krylov)
    part = part + swap(part, blocks, rads, 1, 0)
    chips = blocks // 2 * rads
    parts = lax.all_to_all(
        jnp.broadcast_to(part[None], (chips,) + part.shape), ("chip", "rad"), 0, 0
    )
    basis, coefficients, upper = finish(blocks * width, parts, g, x, krylov)
    return (basis, coefficients.T, upper)


def solution(mesh):
    blocks, rads = mesh.shape["ax"], mesh.shape["rad"]
    split = Mesh(mesh.devices.reshape(blocks // 2, 2, rads), ALL)
    ax = ("chip", "core")
    return jax.shard_map(
        step,
        mesh=split,
        in_specs=(
            P(ax, None, "rad", None),
            P(ax, "rad", None),
            P(ax, None, None, None),
            P(ax, None, "rad"),
        ),
        out_specs=(P(ax, None, "rad"), P(), P()),
        check_vma=False,
    )
```

```python
import functools

import jax
import jax.numpy as jnp
from jax import lax
from jax.experimental import pallas as pl
from jax.experimental.pallas import tpu as pltpu
from jax.sharding import Mesh
from jax.sharding import PartitionSpec as P

NRHS = 16
precise = lax.Precision.HIGHEST


VMEM = pl.BlockSpec(memory_space=pltpu.VMEM)
SMEM = pl.BlockSpec(memory_space=pltpu.SMEM)
ANY = pl.BlockSpec(memory_space=pl.ANY)


def near(value):
    return pltpu.with_memory_space_constraint(value, pltpu.VMEM)


def far(value):
    return pltpu.with_memory_space_constraint(value, pltpu.HBM)


def made(shape, dtype=jnp.float32):
    return pltpu.VMEM(shape, dtype)


def nt_dot(a, b, precision=None):
    return lax.dot_general(
        a, b, (((1,), (1,)), ((), ())), precision=precision,
        preferred_element_type=jnp.float32,
    )


def nn_dot(a, b, precision=None):
    return lax.dot_general(
        a, b, (((1,), (0,)), ((), ())), precision=precision,
        preferred_element_type=jnp.float32,
    )


def split2(value):
    high = value.astype(jnp.bfloat16)
    low = (value - high.astype(jnp.float32)).astype(jnp.bfloat16)
    return high, low


def masks_kernel(pattern_ref, out_ref):
    spanned, kinds_pad, width = out_ref.shape
    fields, _, _, kinds = pattern_ref.shape
    points = width // fields
    first = lax.axis_index("rad") * (width // lax.axis_size("rad")) // points
    col_field = lax.broadcasted_iota(jnp.int32, (kinds_pad, width), 1) // points
    for local in range(spanned):
        field = jnp.minimum(first + local, fields - 1)
        rows = [pattern_ref[field, col, :, :].astype(jnp.float32) for col in range(fields)]
        table = jnp.concatenate(rows, axis=0)
        table = jnp.concatenate(
            [table, jnp.zeros((fields, 128 - kinds), jnp.float32)], axis=1
        )
        table = jnp.concatenate([table, jnp.zeros((16 - fields, 128), jnp.float32)], axis=0)
        by_kind = table.T[:kinds_pad]
        keep = jnp.zeros((kinds_pad, width), jnp.float32)
        for col in range(fields):
            keep = jnp.where(col_field == col, by_kind[:, col : col + 1], keep)
        out_ref[local] = keep


def make_masks(pattern, rows, width):
    fields, _, _, _ = pattern.shape
    spanned = rows // (width // fields) + 1
    return pl.pallas_call(
        masks_kernel,
        out_shape=made((spanned, 16, width)),
        in_specs=[VMEM],
        out_specs=VMEM,
        compiler_params=pltpu.CompilerParams(vmem_limit_bytes=4 << 20),
        name="masks",
    )(near(pattern))


def kind_of(rung, slot):
    odd = (lax.axis_index(("chip", "core")) // (1 << rung)) % 2
    return 2 * rung + (odd if slot == 0 else 1 - odd)


def fetch_kernel(rung, slots, couplings_ref, *rest):
    out_ref, sems = rest[-2:]
    copies = []
    for slot in range(slots):
        copy = pltpu.make_async_copy(
            couplings_ref.at[0, kind_of(rung, slot)], out_ref.at[slot], sems.at[slot]
        )
        copy.start(priority=slot)
        copies.append(copy)
    for copy in copies:
        copy.wait()


def fetch(rung, slots, couplings, after=None):
    rows, width = couplings.shape[2:]
    args = (far(couplings),) if after is None else (far(couplings), near(after))
    return pl.pallas_call(
        functools.partial(fetch_kernel, rung, slots),
        out_shape=made((slots, rows, width), jnp.bfloat16),
        in_specs=[ANY, VMEM][: len(args)],
        out_specs=VMEM,
        scratch_shapes=[pltpu.SemaphoreType.DMA((slots,))],
        compiler_params=pltpu.CompilerParams(vmem_limit_bytes=4 << 20),
    )(*args)


def pivot_kernel(pivots_ref, _, out_ref, stage, sems):
    rows = pivots_ref.shape[1]
    part = rows // 3
    copies = []
    for i in range(3):
        copy = pltpu.make_async_copy(
            pivots_ref.at[0, pl.ds(i * part, part)], stage.at[pl.ds(i * part, part)], sems.at[i]
        )
        copy.start(priority=i % 2)
        copies.append(copy)
    for i, copy in enumerate(copies):
        copy.wait()
        for tile in range(part // 16):
            at = pl.ds(i * part + tile * 16, 16)
            high, low = split2(stage[at, :])
            out_ref[0, at, :] = high
            out_ref[1, at, :] = low


def prep_pivots(pivots, after):
    rows, width = pivots.shape[1:]
    return pl.pallas_call(
        pivot_kernel,
        out_shape=made((2, rows, width), jnp.bfloat16),
        in_specs=[ANY, VMEM],
        out_specs=VMEM,
        scratch_shapes=[pltpu.VMEM((rows, width), jnp.float32), pltpu.SemaphoreType.DMA((3,))],
        compiler_params=pltpu.CompilerParams(vmem_limit_bytes=8 << 20),
        name="prep_pivots",
    )(far(pivots), near(after))


def gather_rows(slices, whole):
    rad = lax.axis_index("rad")
    for m, piece in enumerate(slices):
        first = piece.shape[0] - NRHS if piece.shape[0] > NRHS + 8 else 0
        whole[rad ^ m] = piece[first : first + NRHS, :]
    v = jnp.concatenate([whole[t] for t in range(4)], axis=1)
    return jnp.concatenate(split2(v), axis=0)


OUTER = ((0, (("s", 0), 80)), (1280, (16, ("s", 3))))
INNER = ((384, (48, ("s", 1), ("s", 2), 112)),)


def half_push(kind, points, ranges, w_ref, slot, masks_ref, whole):
    spanned = masks_ref.shape[0]
    rows = w_ref.shape[1]
    product = None
    for start, items in ranges:
        pieces = [
            whole[item[1]] if isinstance(item, tuple) else jnp.zeros((NRHS, item), jnp.float32)
            for item in items
        ]
        lhs = jnp.concatenate(split2(jnp.concatenate(pieces, axis=1)), axis=0)
        size = lhs.shape[1]
        parts = []
        for local in range(spanned):
            keep = masks_ref[local, pl.ds(kind, 1), start : start + size]
            keep = jnp.broadcast_to(keep, (16, size)).astype(jnp.bfloat16)
            parts.append(lhs * jnp.concatenate([keep, keep], axis=0))
        one = nt_dot(jnp.concatenate(parts, axis=0), w_ref[slot, :, start : start + size])
        product = one if product is None else product + one
    offset = lax.axis_index("rad") * rows
    first = offset // points
    row = offset + lax.broadcasted_iota(jnp.int32, (NRHS, rows), 1)
    push = None
    for local in reversed(range(spanned)):
        at = 2 * NRHS * local
        one = product[at : at + NRHS] + product[at + NRHS : at + 2 * NRHS]
        push = one if push is None else jnp.where(row < (first + local + 1) * points, one, push)
    return push


def near_half_kernel(rung, slots, points, s0, s3, w_ref, masks_ref, *rest):
    outs, whole = rest[:-1], rest[-1]
    rad = lax.axis_index("rad")
    for m, piece in ((0, s0), (3, s3)):
        whole[rad ^ m] = piece[piece.shape[0] - NRHS :, :]
    if len(outs) > slots:
        stored = s0[...]
        product = nt_dot(stored, stored, precise)
        outs[slots][...] = jnp.concatenate([product[8 * i : 8 * i + 8] for i in range(4)], axis=1)

    def run(ranges):
        for slot in range(slots):
            outs[slot][...] = half_push(
                kind_of(rung, slot), points, ranges, w_ref, slot, masks_ref, whole
            )

    edge = (rad == 0) | (rad == 3)
    pl.when(edge)(lambda: run(OUTER))
    pl.when(jnp.logical_not(edge))(lambda: run(INNER))


def far_half_kernel(rung, slots, points, s1, s2, w_ref, masks_ref, g_ref, *rest):
    halves, outs, whole = rest[:slots], rest[slots:-1], rest[-1]
    rad = lax.axis_index("rad")
    for m, piece in ((1, s1), (2, s2)):
        whole[rad ^ m] = piece[piece.shape[0] - NRHS :, :]

    def run(ranges):
        for slot in range(slots):
            push = half_push(kind_of(rung, slot), points, ranges, w_ref, slot, masks_ref, whole)
            outs[slot][:NRHS, :] = push + halves[slot][...]

    edge = (rad == 0) | (rad == 3)
    pl.when(edge)(lambda: run(INNER))
    pl.when(jnp.logical_not(edge))(lambda: run(OUTER))
    outs[0][NRHS:, :128] = g_ref[...]
    outs[0][NRHS:, 128:] = jnp.zeros((8, outs[0].shape[1] - 128), jnp.float32)


def near_half(rung, slots, points, own, third, weights, masks):
    rows = weights.shape[1]
    shapes = [(NRHS, rows)] * slots + [(8, 128)] * (rung == 0)
    return pl.pallas_call(
        functools.partial(near_half_kernel, rung, slots, points),
        out_shape=[made(s) for s in shapes],
        in_specs=[VMEM] * 4,
        out_specs=[VMEM] * len(shapes),
        scratch_shapes=[pltpu.VMEM((4, NRHS, rows), jnp.float32)],
        compiler_params=pltpu.CompilerParams(vmem_limit_bytes=4 << 20),
        name="nearhalf",
    )(*map(near, (own, third, weights, masks)))


def level(rung, slots, points, slices, weights, masks, g, halves):
    rows = weights.shape[1]
    args = (slices[1], slices[2], weights, masks, g, *halves)
    shapes = [(NRHS + 8, rows), (NRHS, rows)][:slots]
    return pl.pallas_call(
        functools.partial(far_half_kernel, rung, slots, points),
        out_shape=[made(s) for s in shapes],
        in_specs=[VMEM] * len(args),
        out_specs=[VMEM] * slots,
        scratch_shapes=[pltpu.VMEM((4, NRHS, rows), jnp.float32)],
        compiler_params=pltpu.CompilerParams(vmem_limit_bytes=4 << 20),
        name="level",
    )(*map(near, args))


def solve_kernel(s0, s1, s2, s3, p_ref, stored_ref, x_ref, part_ref, g_ref, whole, gs):
    rad = lax.axis_index("rad")
    lhs = gather_rows((s0, s1, s2, s3), whole)
    both = nt_dot(lhs, p_ref[0])
    x = both[:NRHS] + both[NRHS:] + nt_dot(lhs[:NRHS], p_ref[1])
    x_ref[...] = x
    t = jnp.concatenate(
        [nt_dot(x, stored_ref[0], precise), nt_dot(x, x, precise)], axis=1
    )
    part_ref[...] = jnp.concatenate(
        [t[:8], t[8:], jnp.zeros((8, 32), jnp.float32)], axis=1
    )
    for m, piece in enumerate((s0, s1, s2, s3)):
        gs[rad ^ m] = piece[NRHS:, :128]
    g_ref[...] = (gs[0] + gs[1]) + (gs[2] + gs[3])


def solve(slices, pivots, krylov):
    rows = pivots.shape[1]
    return pl.pallas_call(
        solve_kernel,
        out_shape=[
            made((NRHS, rows)),
            made((8, 128)),
            made((8, 128)),
        ],
        in_specs=[VMEM] * 6,
        out_specs=[VMEM] * 3,
        scratch_shapes=[
            pltpu.VMEM((4, NRHS, rows), jnp.float32),
            pltpu.VMEM((4, 8, 128), jnp.float32),
        ],
        compiler_params=pltpu.CompilerParams(vmem_limit_bytes=8 << 20),
        name="solve",
    )(*map(near, (*slices, pivots, krylov)))


def finish_kernel(total, parts_ref, g_ref, x_ref, stored_ref, basis_ref, coef_ref, upper_ref):
    s = jnp.sum(parts_ref[...], axis=0) * (1.0 / total)
    t = jnp.concatenate([s[:, :48], s[:, 48:96]], axis=0)
    gs = g_ref[...] * (1.0 / total)
    g = jnp.concatenate([gs[:, 32 * i : 32 * i + 32] for i in range(4)], axis=0)
    ct = t[:, :32]
    xx = t[:, 32:48]
    coef_ref[...] = ct
    stored = stored_ref[0]
    remainder = x_ref[...] - nn_dot(ct, stored, precise)
    gram = xx - nt_dot(2.0 * ct - nn_dot(ct, g, precise), ct, precise)
    sub = lax.broadcasted_iota(jnp.int32, (NRHS, 128), 0)
    lane = lax.broadcasted_iota(jnp.int32, (NRHS, 128), 1)
    rows = [jnp.broadcast_to(gram[:, i : i + 1], (NRHS, 128)) for i in range(NRHS)]
    for k in range(NRHS - 1):
        inverse = 1.0 / rows[k][k : k + 1, :]
        at_pivot = sub == k
        pivot_row = jnp.where(at_pivot, 1.0, rows[k])
        for i in range(k + 1, NRHS):
            factor = rows[i][k : k + 1, :] * inverse
            rows[i] = jnp.where(at_pivot, 0.0, rows[i]) - factor * pivot_row
    packed = rows[0]
    for i in range(1, NRHS):
        packed = jnp.where(lane == i, rows[i], packed)
    on_diag = sub == lane
    diag = jnp.sum(jnp.where(on_diag, packed, 0.0), axis=0, keepdims=True)
    scale = lax.rsqrt(jnp.where(lane[:1] < NRHS, diag, 1.0))
    lower = jnp.where(sub >= lane, packed, 0.0) * scale
    inverse_t = jnp.where(on_diag, 1.0, jnp.where(sub < lane, packed, 0.0)) * scale
    upper_ref[...] = lower.T[:NRHS, :]
    basis_ref[0] = nn_dot(inverse_t.T[:NRHS, :], remainder, precise)


def finish(total, parts, g, x, krylov):
    rows = x.shape[1]
    stored = krylov.shape[1]
    return pl.pallas_call(
        functools.partial(finish_kernel, total),
        out_shape=[
            jax.ShapeDtypeStruct((1, NRHS, rows), jnp.float32),
            jax.ShapeDtypeStruct((NRHS, stored), jnp.float32),
            jax.ShapeDtypeStruct((NRHS, NRHS), jnp.float32),
        ],
        in_specs=[VMEM] * 4,
        out_specs=[VMEM] * 3,
        compiler_params=pltpu.CompilerParams(vmem_limit_bytes=8 << 20),
        name="finish",
    )(*map(near, (parts, g, x, krylov)))


ALL = ("chip", "core", "rad")


def swap(value, blocks, rads, stride, parity):
    pairs = []
    for a in range(blocks):
        up = ((a // stride) + parity) % 2 == 0
        b = (a + stride if up else a - stride) % blocks
        pairs += [(a * rads + r, b * rads + r) for r in range(rads)]
    return lax.ppermute(value, ALL, pairs)


def gather(value, blocks, rads):
    out = [value]
    for m in range(1, rads):
        pairs = [(a * rads + r, a * rads + (r ^ m)) for a in range(blocks) for r in range(rads)]
        out.append(lax.ppermute(value, ALL, pairs))
    return out


def step(couplings, pivots, pattern, krylov):
    width = couplings.shape[3]
    blocks = lax.axis_size("chip") * lax.axis_size("core")
    rads = lax.axis_size("rad")
    levels = blocks.bit_length() - 1
    block = lax.axis_index(("chip", "core"))
    pattern = pattern.transpose(2, 3, 0, 1)
    slices = gather(krylov[0], blocks, rads)
    weights = fetch(0, 2, couplings)
    masks = make_masks(pattern, couplings.shape[2], width)
    points = width // pattern.shape[0]
    residue = krylov[0, krylov.shape[1] - NRHS :, :]
    for rung in range(levels):
        stride = 1 << rung
        last = rung == levels - 1
        slots = 1 if last else 2
        halves = near_half(rung, slots, points, slices[0], slices[3], weights, masks)
        if rung == 0:
            g = halves[slots]
        sent = level(rung, slots, points, slices, weights, masks, g, halves[:slots])
        if not last:
            weights = fetch(rung + 1, 1 if rung + 2 == levels else 2, couplings, sent[0])
        got = swap(sent[0], blocks, rads, stride, 0)
        other = None if last else swap(sent[1], blocks, rads, stride, 1)
        residue = residue - got[:NRHS]
        g = g + got[NRHS:, :128]
        if not last:
            place = block // stride
            inside = jnp.where(place % 2 == 0, place > 0, place < blocks // stride - 1)
            residue = residue - jnp.where(inside, other, 0.0)
            payload = residue
        else:
            tail = jnp.pad(g, ((0, 0), (0, residue.shape[1] - 128)))
            payload = jnp.concatenate([residue, tail], axis=0)
        slices = gather(payload, blocks, rads)
        if last:
            weights = prep_pivots(pivots, payload)
    x, part, g = solve(slices, weights, krylov)
    part = part + swap(part, blocks, rads, 1, 0)
    chips = blocks // 2 * rads
    parts = lax.all_to_all(
        jnp.broadcast_to(part[None], (chips,) + part.shape), ("chip", "rad"), 0, 0
    )
    basis, coefficients, upper = finish(blocks * width, parts, g, x, krylov)
    return (basis, coefficients.T, upper)


def solution(mesh):
    blocks, rads = mesh.shape["ax"], mesh.shape["rad"]
    split = Mesh(mesh.devices.reshape(blocks // 2, 2, rads), ALL)
    ax = ("chip", "core")
    return jax.shard_map(
        step,
        mesh=split,
        in_specs=(
            P(ax, None, "rad", None),
            P(ax, "rad", None),
            P(ax, None, None, None),
            P(ax, None, "rad"),
        ),
        out_specs=(P(ax, None, "rad"), P(), P()),
        check_vma=False,
    )
```

```python
import functools

import jax
import jax.numpy as jnp
from jax import lax
from jax.experimental import pallas as pl
from jax.experimental.pallas import tpu as pltpu
from jax.sharding import Mesh
from jax.sharding import PartitionSpec as P

NRHS = 16
precise = lax.Precision.HIGHEST


VMEM = pl.BlockSpec(memory_space=pltpu.VMEM)
SMEM = pl.BlockSpec(memory_space=pltpu.SMEM)
ANY = pl.BlockSpec(memory_space=pl.ANY)


def near(value):
    return pltpu.with_memory_space_constraint(value, pltpu.VMEM)


def far(value):
    return pltpu.with_memory_space_constraint(value, pltpu.HBM)


def made(shape, dtype=jnp.float32):
    return pltpu.VMEM(shape, dtype)


def nt_dot(a, b, precision=None):
    return lax.dot_general(
        a, b, (((1,), (1,)), ((), ())), precision=precision,
        preferred_element_type=jnp.float32,
    )


def nn_dot(a, b, precision=None):
    return lax.dot_general(
        a, b, (((1,), (0,)), ((), ())), precision=precision,
        preferred_element_type=jnp.float32,
    )


def split2(value):
    high = value.astype(jnp.bfloat16)
    low = (value - high.astype(jnp.float32)).astype(jnp.bfloat16)
    return high, low


def masks_kernel(pattern_ref, out_ref):
    spanned, kinds_pad, width = out_ref.shape
    fields, _, _, kinds = pattern_ref.shape
    points = width // fields
    first = lax.axis_index("rad") * (width // lax.axis_size("rad")) // points
    col_field = lax.broadcasted_iota(jnp.int32, (kinds_pad, width), 1) // points
    for local in range(spanned):
        field = jnp.minimum(first + local, fields - 1)
        rows = [pattern_ref[field, col, :, :].astype(jnp.float32) for col in range(fields)]
        table = jnp.concatenate(rows, axis=0)
        table = jnp.concatenate(
            [table, jnp.zeros((fields, 128 - kinds), jnp.float32)], axis=1
        )
        table = jnp.concatenate([table, jnp.zeros((16 - fields, 128), jnp.float32)], axis=0)
        by_kind = table.T[:kinds_pad]
        keep = jnp.zeros((kinds_pad, width), jnp.float32)
        for col in range(fields):
            keep = jnp.where(col_field == col, by_kind[:, col : col + 1], keep)
        out_ref[local] = keep


def make_masks(pattern, rows, width):
    fields, _, _, _ = pattern.shape
    spanned = rows // (width // fields) + 1
    return pl.pallas_call(
        masks_kernel,
        out_shape=made((spanned, 16, width)),
        in_specs=[VMEM],
        out_specs=VMEM,
        compiler_params=pltpu.CompilerParams(vmem_limit_bytes=4 << 20),
        name="masks",
    )(near(pattern))


def kind_of(rung, slot):
    odd = (lax.axis_index(("chip", "core")) // (1 << rung)) % 2
    return 2 * rung + (odd if slot == 0 else 1 - odd)


def fetch_kernel(rung, slots, couplings_ref, *rest):
    out_ref, sems = rest[-2:]
    copies = []
    for slot in range(slots):
        copy = pltpu.make_async_copy(
            couplings_ref.at[0, kind_of(rung, slot)], out_ref.at[slot], sems.at[slot]
        )
        copy.start(priority=slot)
        copies.append(copy)
    for copy in copies:
        copy.wait()


def fetch(rung, slots, couplings, after=None):
    rows, width = couplings.shape[2:]
    args = (far(couplings),) if after is None else (far(couplings), near(after))
    return pl.pallas_call(
        functools.partial(fetch_kernel, rung, slots),
        out_shape=made((slots, rows, width), jnp.bfloat16),
        in_specs=[ANY, VMEM][: len(args)],
        out_specs=VMEM,
        scratch_shapes=[pltpu.SemaphoreType.DMA((slots,))],
        compiler_params=pltpu.CompilerParams(vmem_limit_bytes=4 << 20),
    )(*args)


def pivot_kernel(pivots_ref, _, out_ref, stage, sems):
    rows = pivots_ref.shape[1]
    part = rows // 3
    copies = []
    for i in range(3):
        copy = pltpu.make_async_copy(
            pivots_ref.at[0, pl.ds(i * part, part)], stage.at[pl.ds(i * part, part)], sems.at[i]
        )
        copy.start(priority=i % 2)
        copies.append(copy)
    for i, copy in enumerate(copies):
        copy.wait()
        for tile in range(part // 16):
            at = pl.ds(i * part + tile * 16, 16)
            high, low = split2(stage[at, :])
            out_ref[0, at, :] = high
            out_ref[1, at, :] = low


def prep_pivots(pivots, after):
    rows, width = pivots.shape[1:]
    return pl.pallas_call(
        pivot_kernel,
        out_shape=made((2, rows, width), jnp.bfloat16),
        in_specs=[ANY, VMEM],
        out_specs=VMEM,
        scratch_shapes=[pltpu.VMEM((rows, width), jnp.float32), pltpu.SemaphoreType.DMA((3,))],
        compiler_params=pltpu.CompilerParams(vmem_limit_bytes=8 << 20),
        name="prep_pivots",
    )(far(pivots), near(after))


OUTER = ((0, (("s", 0), 80)), (1280, (16, ("s", 3))))
INNER = ((384, (48, ("s", 1), ("s", 2), 112)),)


def half_push(kind, points, ranges, w_ref, slot, masks_ref, whole):
    spanned = masks_ref.shape[0]
    rows = w_ref.shape[1]
    product = None
    for start, items in ranges:
        pieces = [
            whole[item[1]] if isinstance(item, tuple) else jnp.zeros((NRHS, item), jnp.float32)
            for item in items
        ]
        lhs = jnp.concatenate(split2(jnp.concatenate(pieces, axis=1)), axis=0)
        size = lhs.shape[1]
        parts = []
        for local in range(spanned):
            keep = masks_ref[local, pl.ds(kind, 1), start : start + size]
            keep = jnp.broadcast_to(keep, (16, size)).astype(jnp.bfloat16)
            parts.append(lhs * jnp.concatenate([keep, keep], axis=0))
        one = nt_dot(jnp.concatenate(parts, axis=0), w_ref[slot, :, start : start + size])
        product = one if product is None else product + one
    offset = lax.axis_index("rad") * rows
    first = offset // points
    row = offset + lax.broadcasted_iota(jnp.int32, (NRHS, rows), 1)
    push = None
    for local in reversed(range(spanned)):
        at = 2 * NRHS * local
        one = product[at : at + NRHS] + product[at + NRHS : at + 2 * NRHS]
        push = one if push is None else jnp.where(row < (first + local + 1) * points, one, push)
    return push


def near_half_kernel(rung, slots, points, s0, s3, w_ref, masks_ref, *rest):
    outs, whole = rest[:-1], rest[-1]
    rad = lax.axis_index("rad")
    for m, piece in ((0, s0), (3, s3)):
        whole[rad ^ m] = piece[piece.shape[0] - NRHS :, :]
    if len(outs) > slots:
        stored = s0[...]
        product = nt_dot(stored, stored, precise)
        outs[slots][...] = jnp.concatenate([product[8 * i : 8 * i + 8] for i in range(4)], axis=1)

    def run(ranges):
        for slot in range(slots):
            outs[slot][...] = half_push(
                kind_of(rung, slot), points, ranges, w_ref, slot, masks_ref, whole
            )

    edge = (rad == 0) | (rad == 3)
    pl.when(edge)(lambda: run(OUTER))
    pl.when(jnp.logical_not(edge))(lambda: run(INNER))


def far_half_kernel(rung, slots, points, s1, s2, w_ref, masks_ref, g_ref, *rest):
    halves, outs, whole = rest[:slots], rest[slots:-1], rest[-1]
    rad = lax.axis_index("rad")
    for m, piece in ((1, s1), (2, s2)):
        whole[rad ^ m] = piece[piece.shape[0] - NRHS :, :]

    def run(ranges):
        for slot in range(slots):
            push = half_push(kind_of(rung, slot), points, ranges, w_ref, slot, masks_ref, whole)
            outs[slot][:NRHS, :] = push + halves[slot][...]

    edge = (rad == 0) | (rad == 3)
    pl.when(edge)(lambda: run(INNER))
    pl.when(jnp.logical_not(edge))(lambda: run(OUTER))
    outs[0][NRHS:, :128] = g_ref[...]
    outs[0][NRHS:, 128:] = jnp.zeros((8, outs[0].shape[1] - 128), jnp.float32)


def near_half(rung, slots, points, own, third, weights, masks):
    rows = weights.shape[1]
    shapes = [(NRHS, rows)] * slots + [(8, 128)] * (rung == 0)
    return pl.pallas_call(
        functools.partial(near_half_kernel, rung, slots, points),
        out_shape=[made(s) for s in shapes],
        in_specs=[VMEM] * 4,
        out_specs=[VMEM] * len(shapes),
        scratch_shapes=[pltpu.VMEM((4, NRHS, rows), jnp.float32)],
        compiler_params=pltpu.CompilerParams(vmem_limit_bytes=4 << 20),
        name="nearhalf",
    )(*map(near, (own, third, weights, masks)))


def level(rung, slots, points, slices, weights, masks, g, halves):
    rows = weights.shape[1]
    args = (slices[1], slices[2], weights, masks, g, *halves)
    shapes = [(NRHS + 8, rows), (NRHS, rows)][:slots]
    return pl.pallas_call(
        functools.partial(far_half_kernel, rung, slots, points),
        out_shape=[made(s) for s in shapes],
        in_specs=[VMEM] * len(args),
        out_specs=[VMEM] * slots,
        scratch_shapes=[pltpu.VMEM((4, NRHS, rows), jnp.float32)],
        compiler_params=pltpu.CompilerParams(vmem_limit_bytes=4 << 20),
        name="level",
    )(*map(near, args))


def half_solution(ranges, p_ref, whole):
    x = None
    for start, items in ranges:
        pieces = [
            whole[item[1]] if isinstance(item, tuple) else jnp.zeros((NRHS, item), jnp.float32)
            for item in items
        ]
        lhs = jnp.concatenate(split2(jnp.concatenate(pieces, axis=1)), axis=0)
        size = lhs.shape[1]
        both = nt_dot(lhs, p_ref[0, :, start : start + size])
        one = both[:NRHS] + both[NRHS:] + nt_dot(lhs[:NRHS], p_ref[1, :, start : start + size])
        x = one if x is None else x + one
    return x


def near_solve_kernel(s0, s3, p_ref, half_ref, whole):
    rad = lax.axis_index("rad")
    whole[rad] = s0[:NRHS, :]
    whole[rad ^ 3] = s3[:NRHS, :]

    def run(ranges):
        half_ref[...] = half_solution(ranges, p_ref, whole)

    edge = (rad == 0) | (rad == 3)
    pl.when(edge)(lambda: run(OUTER))
    pl.when(jnp.logical_not(edge))(lambda: run(INNER))


def near_solve(own, third, pivots):
    rows = pivots.shape[1]
    return pl.pallas_call(
        near_solve_kernel,
        out_shape=made((NRHS, rows)),
        in_specs=[VMEM] * 3,
        out_specs=VMEM,
        scratch_shapes=[pltpu.VMEM((4, NRHS, rows), jnp.float32)],
        compiler_params=pltpu.CompilerParams(vmem_limit_bytes=4 << 20),
        name="nearsolve",
    )(*map(near, (own, third, pivots)))


def solve_kernel(s0, s1, s2, s3, p_ref, stored_ref, half_ref, x_ref, part_ref, g_ref, whole, gs):
    rad = lax.axis_index("rad")
    whole[rad ^ 1] = s1[:NRHS, :]
    whole[rad ^ 2] = s2[:NRHS, :]

    def run(ranges):
        x_ref[...] = half_ref[...] + half_solution(ranges, p_ref, whole)

    edge = (rad == 0) | (rad == 3)
    pl.when(edge)(lambda: run(INNER))
    pl.when(jnp.logical_not(edge))(lambda: run(OUTER))
    for m, piece in enumerate((s0, s1, s2, s3)):
        gs[rad ^ m] = piece[NRHS:, :128]
    x = x_ref[...]
    t = nt_dot(x, jnp.concatenate([stored_ref[0], x], axis=0), precise)
    part_ref[...] = jnp.concatenate(
        [t[:8], t[8:], jnp.zeros((8, 32), jnp.float32)], axis=1
    )
    g_ref[...] = (gs[0] + gs[1]) + (gs[2] + gs[3])


def solve(slices, pivots, krylov, half):
    rows = pivots.shape[1]
    return pl.pallas_call(
        solve_kernel,
        out_shape=[
            made((NRHS, rows)),
            made((8, 128)),
            made((8, 128)),
        ],
        in_specs=[VMEM] * 7,
        out_specs=[VMEM] * 3,
        scratch_shapes=[
            pltpu.VMEM((4, NRHS, rows), jnp.float32),
            pltpu.VMEM((4, 8, 128), jnp.float32),
        ],
        compiler_params=pltpu.CompilerParams(vmem_limit_bytes=8 << 20),
        name="solve",
    )(*map(near, (*slices, pivots, krylov, half)))


def finish_kernel(total, parts_ref, g_ref, x_ref, stored_ref, basis_ref, coef_ref, upper_ref):
    s = jnp.sum(parts_ref[...], axis=0) * (1.0 / total)
    t = jnp.concatenate([s[:, :48], s[:, 48:96]], axis=0)
    gs = g_ref[...] * (1.0 / total)
    g = jnp.concatenate([gs[:, 32 * i : 32 * i + 32] for i in range(4)], axis=0)
    ct = t[:, :32]
    xx = t[:, 32:48]
    coef_ref[...] = ct
    stored = stored_ref[0]
    remainder = x_ref[...] - nn_dot(ct, stored, precise)
    gram = xx - nt_dot(2.0 * ct - nn_dot(ct, g, precise), ct, precise)
    sub = lax.broadcasted_iota(jnp.int32, (NRHS, 128), 0)
    lane = lax.broadcasted_iota(jnp.int32, (NRHS, 128), 1)
    rows = [jnp.broadcast_to(gram[:, i : i + 1], (NRHS, 128)) for i in range(NRHS)]
    for k in range(NRHS - 1):
        inverse = 1.0 / rows[k][k : k + 1, :]
        at_pivot = sub == k
        pivot_row = jnp.where(at_pivot, 1.0, rows[k])
        for i in range(k + 1, NRHS):
            factor = rows[i][k : k + 1, :] * inverse
            rows[i] = jnp.where(at_pivot, 0.0, rows[i]) - factor * pivot_row
    packed = rows[0]
    for i in range(1, NRHS):
        packed = jnp.where(lane == i, rows[i], packed)
    on_diag = sub == lane
    diag = jnp.sum(jnp.where(on_diag, packed, 0.0), axis=0, keepdims=True)
    scale = lax.rsqrt(jnp.where(lane[:1] < NRHS, diag, 1.0))
    lower = jnp.where(sub >= lane, packed, 0.0) * scale
    inverse_t = jnp.where(on_diag, 1.0, jnp.where(sub < lane, packed, 0.0)) * scale
    upper_ref[...] = lower.T[:NRHS, :]
    basis_ref[0] = nn_dot(inverse_t.T[:NRHS, :], remainder, precise)


def finish(total, parts, g, x, krylov):
    rows = x.shape[1]
    stored = krylov.shape[1]
    return pl.pallas_call(
        functools.partial(finish_kernel, total),
        out_shape=[
            jax.ShapeDtypeStruct((1, NRHS, rows), jnp.float32),
            jax.ShapeDtypeStruct((NRHS, stored), jnp.float32),
            jax.ShapeDtypeStruct((NRHS, NRHS), jnp.float32),
        ],
        in_specs=[VMEM] * 4,
        out_specs=[VMEM] * 3,
        compiler_params=pltpu.CompilerParams(vmem_limit_bytes=8 << 20),
        name="finish",
    )(*map(near, (parts, g, x, krylov)))


ALL = ("chip", "core", "rad")


def swap(value, blocks, rads, stride, parity):
    pairs = []
    for a in range(blocks):
        up = ((a // stride) + parity) % 2 == 0
        b = (a + stride if up else a - stride) % blocks
        pairs += [(a * rads + r, b * rads + r) for r in range(rads)]
    return lax.ppermute(value, ALL, pairs)


def gather(value, blocks, rads):
    out = [value]
    for m in range(1, rads):
        pairs = [(a * rads + r, a * rads + (r ^ m)) for a in range(blocks) for r in range(rads)]
        out.append(lax.ppermute(value, ALL, pairs))
    return out


def step(couplings, pivots, pattern, krylov):
    width = couplings.shape[3]
    blocks = lax.axis_size("chip") * lax.axis_size("core")
    rads = lax.axis_size("rad")
    levels = blocks.bit_length() - 1
    block = lax.axis_index(("chip", "core"))
    pattern = pattern.transpose(2, 3, 0, 1)
    slices = gather(krylov[0], blocks, rads)
    weights = fetch(0, 2, couplings)
    masks = make_masks(pattern, couplings.shape[2], width)
    points = width // pattern.shape[0]
    residue = krylov[0, krylov.shape[1] - NRHS :, :]
    for rung in range(levels):
        stride = 1 << rung
        last = rung == levels - 1
        slots = 1 if last else 2
        halves = near_half(rung, slots, points, slices[0], slices[3], weights, masks)
        if rung == 0:
            g = halves[slots]
        sent = level(rung, slots, points, slices, weights, masks, g, halves[:slots])
        if last:
            weights = prep_pivots(pivots, sent[0])
        else:
            weights = fetch(rung + 1, 1 if rung + 2 == levels else 2, couplings, sent[0])
        got = swap(sent[0], blocks, rads, stride, 0)
        other = None if last else swap(sent[1], blocks, rads, stride, 1)
        residue = residue - got[:NRHS]
        g = g + got[NRHS:, :128]
        if not last:
            place = block // stride
            inside = jnp.where(place % 2 == 0, place > 0, place < blocks // stride - 1)
            residue = residue - jnp.where(inside, other, 0.0)
            payload = residue
        else:
            tail = jnp.pad(g, ((0, 0), (0, residue.shape[1] - 128)))
            payload = jnp.concatenate([residue, tail], axis=0)
        slices = gather(payload, blocks, rads)
        if last:
            half = near_solve(slices[0], slices[3], weights)
    x, part, g = solve(slices, weights, krylov, half)
    part = part + swap(part, blocks, rads, 1, 0)
    chips = blocks // 2 * rads
    parts = lax.all_to_all(
        jnp.broadcast_to(part[None], (chips,) + part.shape), ("chip", "rad"), 0, 0
    )
    basis, coefficients, upper = finish(blocks * width, parts, g, x, krylov)
    return (basis, coefficients.T, upper)


def solution(mesh):
    blocks, rads = mesh.shape["ax"], mesh.shape["rad"]
    split = Mesh(mesh.devices.reshape(blocks // 2, 2, rads), ALL)
    ax = ("chip", "core")
    return jax.shard_map(
        step,
        mesh=split,
        in_specs=(
            P(ax, None, "rad", None),
            P(ax, "rad", None),
            P(ax, None, None, None),
            P(ax, None, "rad"),
        ),
        out_specs=(P(ax, None, "rad"), P(), P()),
        check_vma=False,
    )
```

```python
import functools

import jax
import jax.numpy as jnp
from jax import lax
from jax.experimental import pallas as pl
from jax.experimental.pallas import tpu as pltpu
from jax.sharding import Mesh
from jax.sharding import PartitionSpec as P

NRHS = 16
precise = lax.Precision.HIGHEST


VMEM = pl.BlockSpec(memory_space=pltpu.VMEM)
SMEM = pl.BlockSpec(memory_space=pltpu.SMEM)
ANY = pl.BlockSpec(memory_space=pl.ANY)


def near(value):
    return pltpu.with_memory_space_constraint(value, pltpu.VMEM)


def far(value):
    return pltpu.with_memory_space_constraint(value, pltpu.HBM)


def made(shape, dtype=jnp.float32):
    return pltpu.VMEM(shape, dtype)


def nt_dot(a, b, precision=None):
    return lax.dot_general(
        a, b, (((1,), (1,)), ((), ())), precision=precision,
        preferred_element_type=jnp.float32,
    )


def nn_dot(a, b, precision=None):
    return lax.dot_general(
        a, b, (((1,), (0,)), ((), ())), precision=precision,
        preferred_element_type=jnp.float32,
    )


def split2(value):
    high = value.astype(jnp.bfloat16)
    low = (value - high.astype(jnp.float32)).astype(jnp.bfloat16)
    return high, low


def masks_kernel(pattern_ref, out_ref):
    spanned, _, kinds_pad, width = out_ref.shape
    fields, _, _, kinds = pattern_ref.shape
    points = width // fields
    first = lax.axis_index("rad") * (width // lax.axis_size("rad")) // points
    col_field = lax.broadcasted_iota(jnp.int32, (kinds_pad, width), 1) // points
    for local in range(spanned):
        field = jnp.minimum(first + local, fields - 1)
        rows = [pattern_ref[field, col, :, :].astype(jnp.float32) for col in range(fields)]
        table = jnp.concatenate(rows, axis=0)
        table = jnp.concatenate(
            [table, jnp.zeros((fields, 128 - kinds), jnp.float32)], axis=1
        )
        table = jnp.concatenate([table, jnp.zeros((16 - fields, 128), jnp.float32)], axis=0)
        by_kind = table.T[:kinds_pad]
        keep = jnp.zeros((kinds_pad, width), jnp.float32)
        for col in range(fields):
            keep = jnp.where(col_field == col, by_kind[:, col : col + 1], keep)
        for kind in range(kinds):
            line = jnp.broadcast_to(keep[kind : kind + 1, :], (16, width))
            out_ref[local, kind] = line.astype(jnp.bfloat16)


def make_masks(pattern, rows, width):
    fields, _, _, kinds = pattern.shape
    spanned = rows // (width // fields) + 1
    return pl.pallas_call(
        masks_kernel,
        out_shape=made((spanned, kinds, 16, width), jnp.bfloat16),
        in_specs=[VMEM],
        out_specs=VMEM,
        compiler_params=pltpu.CompilerParams(vmem_limit_bytes=4 << 20),
        name="masks",
    )(near(pattern))


def kind_of(rung, slot):
    odd = (lax.axis_index(("chip", "core")) // (1 << rung)) % 2
    return 2 * rung + (odd if slot == 0 else 1 - odd)


def fetch_kernel(rung, slots, couplings_ref, *rest):
    out_ref, sems = rest[-2:]
    copies = []
    for slot in range(slots):
        copy = pltpu.make_async_copy(
            couplings_ref.at[0, kind_of(rung, slot)], out_ref.at[slot], sems.at[slot]
        )
        copy.start(priority=slot)
        copies.append(copy)
    for copy in copies:
        copy.wait()


def fetch(rung, slots, couplings, after=None):
    rows, width = couplings.shape[2:]
    args = (far(couplings),) if after is None else (far(couplings), near(after))
    return pl.pallas_call(
        functools.partial(fetch_kernel, rung, slots),
        out_shape=made((slots, rows, width), jnp.bfloat16),
        in_specs=[ANY, VMEM][: len(args)],
        out_specs=VMEM,
        scratch_shapes=[pltpu.SemaphoreType.DMA((slots,))],
        compiler_params=pltpu.CompilerParams(vmem_limit_bytes=4 << 20),
    )(*args)


def pivot_kernel(pivots_ref, _, out_ref, stage, sems):
    rows = pivots_ref.shape[1]
    part = rows // 3
    copies = []
    for i in range(3):
        copy = pltpu.make_async_copy(
            pivots_ref.at[0, pl.ds(i * part, part)], stage.at[pl.ds(i * part, part)], sems.at[i]
        )
        copy.start(priority=i % 2)
        copies.append(copy)
    for i, copy in enumerate(copies):
        copy.wait()
        for tile in range(part // 16):
            at = pl.ds(i * part + tile * 16, 16)
            high, low = split2(stage[at, :])
            out_ref[0, at, :] = high
            out_ref[1, at, :] = low


def prep_pivots(pivots, after):
    rows, width = pivots.shape[1:]
    return pl.pallas_call(
        pivot_kernel,
        out_shape=made((2, rows, width), jnp.bfloat16),
        in_specs=[ANY, VMEM],
        out_specs=VMEM,
        scratch_shapes=[pltpu.VMEM((rows, width), jnp.float32), pltpu.SemaphoreType.DMA((3,))],
        compiler_params=pltpu.CompilerParams(vmem_limit_bytes=8 << 20),
        name="prep_pivots",
    )(far(pivots), near(after))


OUTER = ((0, (("s", 0), 80)), (1280, (16, ("s", 3))))
INNER = ((384, (48, ("s", 1), ("s", 2), 112)),)


def half_push(kind, points, ranges, w_ref, slot, masks_ref, whole):
    spanned = masks_ref.shape[0]
    rows = w_ref.shape[1]
    product = None
    for start, items in ranges:
        pieces = [
            whole[item[1]] if isinstance(item, tuple) else jnp.zeros((NRHS, item), jnp.float32)
            for item in items
        ]
        lhs = jnp.concatenate(split2(jnp.concatenate(pieces, axis=1)), axis=0)
        size = lhs.shape[1]
        parts = []
        for local in range(spanned):
            keep = masks_ref[local, kind, :, start : start + size]
            parts.append(lhs * jnp.concatenate([keep, keep], axis=0))
        one = nt_dot(jnp.concatenate(parts, axis=0), w_ref[slot, :, start : start + size])
        product = one if product is None else product + one
    offset = lax.axis_index("rad") * rows
    first = offset // points
    row = offset + lax.broadcasted_iota(jnp.int32, (NRHS, rows), 1)
    push = None
    for local in reversed(range(spanned)):
        at = 2 * NRHS * local
        one = product[at : at + NRHS] + product[at + NRHS : at + 2 * NRHS]
        push = one if push is None else jnp.where(row < (first + local + 1) * points, one, push)
    return push


def near_half_kernel(rung, slots, points, s0, s3, w_ref, masks_ref, *rest):
    outs, whole = rest[:-1], rest[-1]
    rad = lax.axis_index("rad")
    for m, piece in ((0, s0), (3, s3)):
        whole[rad ^ m] = piece[piece.shape[0] - NRHS :, :]
    if len(outs) > slots:
        stored = s0[...]
        product = nt_dot(stored, stored, precise)
        outs[slots][...] = jnp.concatenate([product[8 * i : 8 * i + 8] for i in range(4)], axis=1)

    def run(ranges):
        for slot in range(slots):
            outs[slot][...] = half_push(
                kind_of(rung, slot), points, ranges, w_ref, slot, masks_ref, whole
            )

    edge = (rad == 0) | (rad == 3)
    pl.when(edge)(lambda: run(OUTER))
    pl.when(jnp.logical_not(edge))(lambda: run(INNER))


def far_half_kernel(rung, slots, points, s1, s2, w_ref, masks_ref, g_ref, *rest):
    halves, outs, whole = rest[:slots], rest[slots:-1], rest[-1]
    rad = lax.axis_index("rad")
    for m, piece in ((1, s1), (2, s2)):
        whole[rad ^ m] = piece[piece.shape[0] - NRHS :, :]

    def run(ranges):
        for slot in range(slots):
            push = half_push(kind_of(rung, slot), points, ranges, w_ref, slot, masks_ref, whole)
            outs[slot][:NRHS, :] = push + halves[slot][...]

    edge = (rad == 0) | (rad == 3)
    pl.when(edge)(lambda: run(INNER))
    pl.when(jnp.logical_not(edge))(lambda: run(OUTER))
    outs[0][NRHS:, :128] = g_ref[...]
    outs[0][NRHS:, 128:] = jnp.zeros((8, outs[0].shape[1] - 128), jnp.float32)


def near_half(rung, slots, points, own, third, weights, masks):
    rows = weights.shape[1]
    shapes = [(NRHS, rows)] * slots + [(8, 128)] * (rung == 0)
    return pl.pallas_call(
        functools.partial(near_half_kernel, rung, slots, points),
        out_shape=[made(s) for s in shapes],
        in_specs=[VMEM] * 4,
        out_specs=[VMEM] * len(shapes),
        scratch_shapes=[pltpu.VMEM((4, NRHS, rows), jnp.float32)],
        compiler_params=pltpu.CompilerParams(vmem_limit_bytes=4 << 20),
        name="nearhalf",
    )(*map(near, (own, third, weights, masks)))


def level(rung, slots, points, slices, weights, masks, g, halves):
    rows = weights.shape[1]
    args = (slices[1], slices[2], weights, masks, g, *halves)
    shapes = [(NRHS + 8, rows), (NRHS, rows)][:slots]
    return pl.pallas_call(
        functools.partial(far_half_kernel, rung, slots, points),
        out_shape=[made(s) for s in shapes],
        in_specs=[VMEM] * len(args),
        out_specs=[VMEM] * slots,
        scratch_shapes=[pltpu.VMEM((4, NRHS, rows), jnp.float32)],
        compiler_params=pltpu.CompilerParams(vmem_limit_bytes=4 << 20),
        name="level",
    )(*map(near, args))


def half_solution(ranges, p_ref, whole):
    x = None
    for start, items in ranges:
        pieces = [
            whole[item[1]] if isinstance(item, tuple) else jnp.zeros((NRHS, item), jnp.float32)
            for item in items
        ]
        lhs = jnp.concatenate(split2(jnp.concatenate(pieces, axis=1)), axis=0)
        size = lhs.shape[1]
        both = nt_dot(lhs, p_ref[0, :, start : start + size])
        one = both[:NRHS] + both[NRHS:] + nt_dot(lhs[:NRHS], p_ref[1, :, start : start + size])
        x = one if x is None else x + one
    return x


def near_solve_kernel(s0, s3, p_ref, half_ref, whole):
    rad = lax.axis_index("rad")
    whole[rad] = s0[:NRHS, :]
    whole[rad ^ 3] = s3[:NRHS, :]

    def run(ranges):
        half_ref[...] = half_solution(ranges, p_ref, whole)

    edge = (rad == 0) | (rad == 3)
    pl.when(edge)(lambda: run(OUTER))
    pl.when(jnp.logical_not(edge))(lambda: run(INNER))


def near_solve(own, third, pivots):
    rows = pivots.shape[1]
    return pl.pallas_call(
        near_solve_kernel,
        out_shape=made((NRHS, rows)),
        in_specs=[VMEM] * 3,
        out_specs=VMEM,
        scratch_shapes=[pltpu.VMEM((4, NRHS, rows), jnp.float32)],
        compiler_params=pltpu.CompilerParams(vmem_limit_bytes=4 << 20),
        name="nearsolve",
    )(*map(near, (own, third, pivots)))


def solve_kernel(s0, s1, s2, s3, p_ref, stored_ref, half_ref, x_ref, part_ref, g_ref, whole, gs):
    rad = lax.axis_index("rad")
    whole[rad ^ 1] = s1[:NRHS, :]
    whole[rad ^ 2] = s2[:NRHS, :]

    def run(ranges):
        x_ref[...] = half_ref[...] + half_solution(ranges, p_ref, whole)

    edge = (rad == 0) | (rad == 3)
    pl.when(edge)(lambda: run(INNER))
    pl.when(jnp.logical_not(edge))(lambda: run(OUTER))
    for m, piece in enumerate((s0, s1, s2, s3)):
        gs[rad ^ m] = piece[NRHS:, :128]
    x = x_ref[...]
    t = nt_dot(x, jnp.concatenate([stored_ref[0], x], axis=0), precise)
    part_ref[...] = jnp.concatenate(
        [t[:8], t[8:], jnp.zeros((8, 32), jnp.float32)], axis=1
    )
    g_ref[...] = (gs[0] + gs[1]) + (gs[2] + gs[3])


def solve(slices, pivots, krylov, half):
    rows = pivots.shape[1]
    return pl.pallas_call(
        solve_kernel,
        out_shape=[
            made((NRHS, rows)),
            made((8, 128)),
            made((8, 128)),
        ],
        in_specs=[VMEM] * 7,
        out_specs=[VMEM] * 3,
        scratch_shapes=[
            pltpu.VMEM((4, NRHS, rows), jnp.float32),
            pltpu.VMEM((4, 8, 128), jnp.float32),
        ],
        compiler_params=pltpu.CompilerParams(vmem_limit_bytes=8 << 20),
        name="solve",
    )(*map(near, (*slices, pivots, krylov, half)))


def finish_kernel(total, parts_ref, g_ref, x_ref, stored_ref, basis_ref, coef_ref, upper_ref):
    s = jnp.sum(parts_ref[...], axis=0) * (1.0 / total)
    t = jnp.concatenate([s[:, :48], s[:, 48:96]], axis=0)
    gs = g_ref[...] * (1.0 / total)
    g = jnp.concatenate([gs[:, 32 * i : 32 * i + 32] for i in range(4)], axis=0)
    ct = t[:, :32]
    xx = t[:, 32:48]
    coef_ref[...] = ct
    stored = stored_ref[0]
    remainder = x_ref[...] - nn_dot(ct, stored, precise)
    gram = xx - nt_dot(2.0 * ct - nn_dot(ct, g, precise), ct, precise)
    sub = lax.broadcasted_iota(jnp.int32, (NRHS, 128), 0)
    lane = lax.broadcasted_iota(jnp.int32, (NRHS, 128), 1)
    rows = [jnp.broadcast_to(gram[:, i : i + 1], (NRHS, 128)) for i in range(NRHS)]
    for k in range(NRHS - 1):
        inverse = 1.0 / rows[k][k : k + 1, :]
        at_pivot = sub == k
        pivot_row = jnp.where(at_pivot, 1.0, rows[k])
        for i in range(k + 1, NRHS):
            factor = rows[i][k : k + 1, :] * inverse
            rows[i] = jnp.where(at_pivot, 0.0, rows[i]) - factor * pivot_row
    packed = rows[0]
    for i in range(1, NRHS):
        packed = jnp.where(lane == i, rows[i], packed)
    on_diag = sub == lane
    diag = jnp.sum(jnp.where(on_diag, packed, 0.0), axis=0, keepdims=True)
    scale = lax.rsqrt(jnp.where(lane[:1] < NRHS, diag, 1.0))
    lower = jnp.where(sub >= lane, packed, 0.0) * scale
    inverse_t = jnp.where(on_diag, 1.0, jnp.where(sub < lane, packed, 0.0)) * scale
    upper_ref[...] = lower.T[:NRHS, :]
    basis_ref[0] = nn_dot(inverse_t.T[:NRHS, :], remainder, precise)


def finish(total, parts, g, x, krylov):
    rows = x.shape[1]
    stored = krylov.shape[1]
    return pl.pallas_call(
        functools.partial(finish_kernel, total),
        out_shape=[
            jax.ShapeDtypeStruct((1, NRHS, rows), jnp.float32),
            jax.ShapeDtypeStruct((NRHS, stored), jnp.float32),
            jax.ShapeDtypeStruct((NRHS, NRHS), jnp.float32),
        ],
        in_specs=[VMEM] * 4,
        out_specs=[VMEM] * 3,
        compiler_params=pltpu.CompilerParams(vmem_limit_bytes=8 << 20),
        name="finish",
    )(*map(near, (parts, g, x, krylov)))


ALL = ("chip", "core", "rad")


def swap(value, blocks, rads, stride, parity):
    pairs = []
    for a in range(blocks):
        up = ((a // stride) + parity) % 2 == 0
        b = (a + stride if up else a - stride) % blocks
        pairs += [(a * rads + r, b * rads + r) for r in range(rads)]
    return lax.ppermute(value, ALL, pairs)


def gather(value, blocks, rads):
    out = [value]
    for m in range(1, rads):
        pairs = [(a * rads + r, a * rads + (r ^ m)) for a in range(blocks) for r in range(rads)]
        out.append(lax.ppermute(value, ALL, pairs))
    return out


def step(couplings, pivots, pattern, krylov):
    width = couplings.shape[3]
    blocks = lax.axis_size("chip") * lax.axis_size("core")
    rads = lax.axis_size("rad")
    levels = blocks.bit_length() - 1
    block = lax.axis_index(("chip", "core"))
    pattern = pattern.transpose(2, 3, 0, 1)
    slices = gather(krylov[0], blocks, rads)
    weights = fetch(0, 2, couplings)
    masks = make_masks(pattern, couplings.shape[2], width)
    points = width // pattern.shape[0]
    residue = krylov[0, krylov.shape[1] - NRHS :, :]
    for rung in range(levels):
        stride = 1 << rung
        last = rung == levels - 1
        slots = 1 if last else 2
        halves = near_half(rung, slots, points, slices[0], slices[3], weights, masks)
        if rung == 0:
            g = halves[slots]
        sent = level(rung, slots, points, slices, weights, masks, g, halves[:slots])
        if last:
            weights = prep_pivots(pivots, sent[0])
        else:
            weights = fetch(rung + 1, 1 if rung + 2 == levels else 2, couplings, sent[0])
        got = swap(sent[0], blocks, rads, stride, 0)
        other = None if last else swap(sent[1], blocks, rads, stride, 1)
        residue = residue - got[:NRHS]
        g = g + got[NRHS:, :128]
        if not last:
            place = block // stride
            inside = jnp.where(place % 2 == 0, place > 0, place < blocks // stride - 1)
            residue = residue - jnp.where(inside, other, 0.0)
            payload = residue
        else:
            tail = jnp.pad(g, ((0, 0), (0, residue.shape[1] - 128)))
            payload = jnp.concatenate([residue, tail], axis=0)
        slices = gather(payload, blocks, rads)
        if last:
            half = near_solve(slices[0], slices[3], weights)
    x, part, g = solve(slices, weights, krylov, half)
    part = part + swap(part, blocks, rads, 1, 0)
    chips = blocks // 2 * rads
    parts = lax.all_to_all(
        jnp.broadcast_to(part[None], (chips,) + part.shape), ("chip", "rad"), 0, 0
    )
    basis, coefficients, upper = finish(blocks * width, parts, g, x, krylov)
    return (basis, coefficients.T, upper)


def solution(mesh):
    blocks, rads = mesh.shape["ax"], mesh.shape["rad"]
    split = Mesh(mesh.devices.reshape(blocks // 2, 2, rads), ALL)
    ax = ("chip", "core")
    return jax.shard_map(
        step,
        mesh=split,
        in_specs=(
            P(ax, None, "rad", None),
            P(ax, "rad", None),
            P(ax, None, None, None),
            P(ax, None, "rad"),
        ),
        out_specs=(P(ax, None, "rad"), P(), P()),
        check_vma=False,
    )
```
